32 devices in a mesh: groups: 2 (over y), particle: 8 (over z, x), tensor: 2 (over core).
Axes of the slice: x: 2, y: 2, z: 4, core: 2. Of those that a mesh axis runs over, the one named last changes fastest.
Arguments:
- prefix_cache: bfloat16 [2, 2048, 1024], P(None, 'groups', 'tensor'), parts along dimension 1, may hold values from -5 to 5
- tail_cache: bfloat16 [2, 128, 128, 1024], P(None, ('groups', 'particle'), None, 'tensor'), parts along dimension 1, may hold values from -5 to 5
- ancestors: int32 [128], P('groups'), parts along dimension 0, may hold values from 0 to 63, as said below
- queries: bfloat16 [4, 128, 8192], P(None, ('groups', 'particle'), 'tensor'), parts along dimension 1, may hold values from -8 to 8
- fresh_kv: bfloat16 [2, 4, 128, 1024], P(None, None, ('groups', 'particle'), 'tensor'), parts along dimension 2, may hold values from -5 to 5
- prompt_ids: int32 [2048], P('groups'), parts along dimension 0, may hold values from 0 to 128255
- sampled_ids: int32 [4, 128], P(None, ('groups', 'particle')), parts along dimension 1, may hold values from 0 to 128255
- twist_table: float32 [128256], replicated, may hold values from -5 to 5
- readout: float32 [8192], P('tensor'), may hold values from -0.3 to 0.3
Outputs:
- attended: bfloat16 [4, 128, 8192], P(None, ('groups', 'particle'), 'tensor'), parts along dimension 1
- twists: float32 [4, 128], P(None, ('groups', 'particle')), parts along dimension 1
The draws below stay inside these ranges and needn't reach their ends.
There are 2 independent parts, one for each index of `groups`. The reference program is written for one: setup_inputs(seed, part) draws one part's arguments, and reference() takes and returns one part's arrays. A program takes and returns all parts, laid end to end along the dimension named above; an argument that names none is the same for every part. Nothing has to cross between parts.
Inputs may be any that keep to these rules, and one draw needn't show every extreme that they name: Particle i's ancestor lies on a device at most 2 indices from its own: |ancestors[i] // 8 - i // 8| <= 2, with equality for some particle.
All inputs are finite; a program needn't handle non-finite values.
Results may differ from the reference program's by a relative error of at most 0.0027.
Values may be sent and summed in bfloat16 or wider, within the bound.
No kernel may reach another device: no remote copies, remote signals or barrier semaphores. Data moves between devices by JAX's collectives and lax.ppermute only.
A program may use at most 64 MiB of HBM per device.

```python
import math
from functools import reduce
import jax
import jax.numpy as jnp
from jax import lax

HEADS = 64
KV_HEADS = 8
HEAD = 128
VOCAB = 128256
PART_DEV = 8
PREFIX = 1024
GEN = 128
STEPS = 4
REACH = 2
PARTICLES = 64


def attention_draw(key):
    key_list = jax.random.split(jax.random.fold_in(key, 23), 3)
    group_size = HEADS // KV_HEADS
    shape_query = (STEPS, PARTICLES, KV_HEADS, group_size, HEAD)
    shape_fresh = (STEPS, PARTICLES, KV_HEADS, HEAD)
    query_base = jnp.clip(jax.random.normal(key_list[0], shape_query, jnp.float32), -5.0, 5.0)
    fresh_keys = jnp.clip(jax.random.normal(key_list[1], shape_fresh, jnp.float32), -5.0, 5.0)
    fresh_vals = jnp.clip(jax.random.normal(key_list[2], shape_fresh, jnp.float32), -5.0, 5.0)
    query_base = jnp.clip(query_base + 0.45 * fresh_keys[:, :, :, None, :], -8.0, 8.0)
    queries = query_base.reshape(STEPS, PARTICLES, HEADS * HEAD)
    fresh = jnp.stack([fresh_keys, fresh_vals]).reshape(2, STEPS, PARTICLES, KV_HEADS * HEAD)
    return (queries, fresh)


def draw_queries(key, part):
    return attention_draw(key)[0].astype(jnp.bfloat16)


def draw_fresh_kv(key, part):
    return attention_draw(key)[1].astype(jnp.bfloat16)


def token_draw(key):
    key_list = jax.random.split(jax.random.fold_in(key, 41), 6)
    positions = jnp.arange(PREFIX)
    prompt = jax.random.randint(key_list[0], (PREFIX,), 0, VOCAB)
    spot_prompt = jax.random.randint(key_list[1], (), 0, PREFIX)
    prompt = jnp.where(positions == spot_prompt, 0, prompt)
    prompt = jnp.where(positions == (spot_prompt + 1) % PREFIX, VOCAB - 1, prompt)
    copy_flag = jax.random.randint(key_list[2], (STEPS, PARTICLES), 0, 2)
    source_pos = jax.random.randint(key_list[3], (STEPS, PARTICLES), 0, PREFIX)
    fresh_tokens = jax.random.randint(key_list[4], (STEPS, PARTICLES), 0, VOCAB)
    sampled = jnp.where(copy_flag == 1, prompt[source_pos], fresh_tokens)
    flat_index = jnp.arange(STEPS * PARTICLES).reshape(STEPS, PARTICLES)
    spot_sample = jax.random.randint(key_list[5], (), 0, STEPS * PARTICLES)
    sampled = jnp.where(flat_index == spot_sample, VOCAB - 1, sampled)
    sampled = jnp.where(flat_index == (spot_sample + 1) % (STEPS * PARTICLES), 0, sampled)
    return (prompt.astype(jnp.int32), sampled.astype(jnp.int32))


def draw_prompt_ids(key, part):
    return token_draw(key)[0]


def draw_sampled_ids(key, part):
    return token_draw(key)[1]


def draw_ancestors(key, part):
    key_list = jax.random.split(jax.random.fold_in(key, 59), 2)
    device_count = PARTICLES // PART_DEV
    index = jnp.arange(PARTICLES)
    device = index // PART_DEV
    jump = jax.random.randint(key_list[0], (PARTICLES,), -REACH, REACH + 1)
    own_slot = jax.random.randint(key_list[1], (PARTICLES,), 0, PART_DEV)
    jump = jnp.where(index == 0, REACH, jump)
    jump = jnp.where(index == REACH * PART_DEV, -REACH, jump)
    own_slot = jnp.where(index == REACH * PART_DEV, 0, own_slot)
    jump = jnp.where(index == PARTICLES - 1, 0, jump)
    own_slot = jnp.where(index == PARTICLES - 1, PART_DEV - 1, own_slot)
    target = jnp.clip(device + jump, 0, device_count - 1)
    return (target * PART_DEV + own_slot).astype(jnp.int32)


def level_of(stream_key, dims, pieces, smallest, high):
    gain, own = 1.0, jax.random.fold_in(stream_key, 6)
    for position, blocks in pieces:
        draws = jnp.exp(jax.random.uniform(jax.random.fold_in(own, position), (blocks,), jnp.float32, smallest / len(pieces), high / len(pieces)))
        gain = gain * jnp.repeat(draws, dims[position] // blocks).reshape([-1 if axis == position else 1 for axis in range(len(dims))])
    return gain


def bell_draw(key, dims, scale, most, cuts=(), held_as=jnp.bfloat16):
    factor_of = level_of(key, dims, cuts, -0.22, 0.18) if cuts else 1.0
    values = jax.random.normal(key, dims, jnp.float32) * scale * factor_of
    return jnp.minimum(jnp.maximum(values, -most), most).astype(held_as)


def setup_inputs(seed: int = 0, part: int = 0) -> dict:
    streams_of = jax.random.split(jax.random.key(seed), 10)
    part_keys = jax.random.split(jax.random.fold_in(streams_of[9], part), 10)
    return {
        "prefix_cache": bell_draw(part_keys[0], (2, PREFIX, KV_HEADS * HEAD), 1.0, 5.0, ((2, 2),)),
        "tail_cache": bell_draw(part_keys[1], (2, PARTICLES, GEN, KV_HEADS * HEAD), 1.0, 5.0, ((1, 8), (3, 2))),
        "ancestors": draw_ancestors(jax.random.fold_in(jax.random.fold_in(streams_of[9], part), 71), part),
        "queries": draw_queries(jax.random.fold_in(jax.random.fold_in(streams_of[9], part), 71), part),
        "fresh_kv": draw_fresh_kv(jax.random.fold_in(jax.random.fold_in(streams_of[9], part), 71), part),
        "prompt_ids": draw_prompt_ids(jax.random.fold_in(jax.random.fold_in(streams_of[9], part), 71), part),
        "sampled_ids": draw_sampled_ids(jax.random.fold_in(jax.random.fold_in(streams_of[9], part), 71), part),
        "twist_table": bell_draw(streams_of[7], (VOCAB,), 1.0, 5.0, (), jnp.float32),
        "readout": bell_draw(streams_of[8], (HEADS * HEAD,), 0.05, 0.3, ((0, 2),), jnp.float32),
    }


NEG_FILL = -1e+30

def finish_block(scores, values, pattern):
    block_max = lax.optimization_barrier(jnp.max(scores, axis=-1))
    expo_terms = jnp.exp(scores - block_max[..., None])
    block_sum = lax.optimization_barrier(jnp.sum(expo_terms, axis=-1))
    weights = lax.optimization_barrier(expo_terms.astype(jnp.bfloat16)).astype(jnp.float32)
    block_out = jnp.einsum(pattern, weights, values.astype(jnp.float32), precision=lax.Precision.HIGHEST)
    return (block_out, block_max, block_sum)

def combine_blocks(blocks):
    overall = reduce(jnp.maximum, [member[1] for member in blocks])
    numerator = sum((jnp.exp(member[1] - overall)[..., None] * member[0] for member in blocks))
    denominator = sum((jnp.exp(member[1] - overall) * member[2] for member in blocks))
    return numerator / denominator[..., None]

def reference(prefix_cache, tail_cache, ancestors, queries, fresh_kv, prompt_ids, sampled_ids, twist_table, readout):
    group_size = HEADS // KV_HEADS
    score_scale = 1.0 / math.sqrt(HEAD)
    prefix_keys = prefix_cache[0].reshape(PREFIX, KV_HEADS, HEAD).astype(jnp.float32)
    prefix_vals = prefix_cache[1].reshape(PREFIX, KV_HEADS, HEAD)
    step_index = jnp.arange(STEPS)
    later_mask = step_index[None, :] > step_index[:, None]

    def one_particle(particle_item):
        query_rows, fresh_rows, parent = particle_item
        tail_rows = lax.dynamic_index_in_dim(tail_cache, parent.astype(jnp.int32), axis=1, keepdims=False)
        query_heads = query_rows.reshape(STEPS, KV_HEADS, group_size, HEAD).astype(jnp.float32)
        tail_keys = tail_rows[0].reshape(GEN, KV_HEADS, HEAD).astype(jnp.float32)
        tail_vals = tail_rows[1].reshape(GEN, KV_HEADS, HEAD)
        fresh_keys = fresh_rows[0].reshape(STEPS, KV_HEADS, HEAD).astype(jnp.float32)
        fresh_vals = fresh_rows[1].reshape(STEPS, KV_HEADS, HEAD)
        prefix_scores = jnp.einsum('tkgh,nkh->tkgn', query_heads, prefix_keys, precision=lax.Precision.HIGHEST) * score_scale
        prefix_part = finish_block(prefix_scores, prefix_vals, 'tkgn,nkh->tkgh')
        tail_scores = jnp.einsum('tkgh,nkh->tkgn', query_heads, tail_keys, precision=lax.Precision.HIGHEST) * score_scale
        inherit_part = finish_block(tail_scores, tail_vals, 'tkgn,nkh->tkgh')
        fresh_scores = jnp.einsum('tkgh,skh->tkgs', query_heads, fresh_keys, precision=lax.Precision.HIGHEST) * score_scale
        fresh_scores = jnp.where(later_mask[:, None, None, :], NEG_FILL, fresh_scores)
        fresh_part = finish_block(fresh_scores, fresh_vals, 'tkgs,skh->tkgh')
        context = combine_blocks([prefix_part, inherit_part, fresh_part])
        return context.reshape(STEPS, HEADS * HEAD)
    context = lax.map(one_particle, (jnp.transpose(queries, (1, 0, 2)), jnp.transpose(fresh_kv, (2, 0, 1, 3)), ancestors))
    context = jnp.transpose(context, (1, 0, 2))
    attended = context.astype(jnp.bfloat16)
    twist_attn = jnp.einsum('tpc,c->tp', context, readout, precision=lax.Precision.HIGHEST)
    repeats = lax.optimization_barrier(jnp.sum((sampled_ids[:, :, None] == prompt_ids[None, None, :]).astype(jnp.int32), axis=-1))
    twists = jnp.take(twist_table, sampled_ids) - 2.0 * repeats.astype(jnp.float32) + twist_attn
    return (attended, twists)
```

```python
import functools
import math

import jax
import jax.numpy as jnp
from jax import lax
from jax.experimental import pallas as pl
from jax.experimental.pallas import tpu as pltpu
from jax.sharding import PartitionSpec as P

HEADS = 64
KV_HEADS = 8
HEAD = 128
REACH = 2
GROUP = HEADS // KV_HEADS
EXPONENT_SCALE = math.log2(math.e) / math.sqrt(HEAD)

NEG_FILL = -1e30
LOG_STEPS = 32.0
LOG_FRACTION = 65534.0
TOP_CODE = 32000.0
TINY = 1e-30

F32 = jnp.float32
BF16 = jnp.bfloat16
VMEM = pltpu.MemorySpace.VMEM
SMEM = pltpu.MemorySpace.SMEM


def exchanges(length):
    found = []
    for reach in range(REACH, 0, -1):
        for parity in (0, 1):
            pairs = []
            for i in range(length - reach):
                if (i // reach) % 2 == parity:
                    pairs += [(i, i + reach), (i + reach, i)]
            found.append((reach, parity, pairs))
    return found


def partner_of(index, reach, parity):
    return jnp.where((index // reach) % 2 == parity, index + reach, index - reach)


def slots_on(ancestors_ref, owner, holder, length, count):
    safe = jnp.clip(owner, 0, length - 1)
    exists = safe == owner
    rows = lax.broadcasted_iota(jnp.int32, (count, 1), 0)
    slots = jnp.full((count, 1), -1, jnp.int32)
    for p in range(count):
        slot = ancestors_ref[safe * count + p] - holder * count
        here = exists & (slot >= 0) & (slot < count)
        slots = jnp.where(rows == p, jnp.where(here, slot, -1), slots)
    return slots


def head_rows(query_ref, base):
    steps = query_ref.shape[0]
    pieces = [
        query_ref[t, :, base + g * HEAD : base + (g + 1) * HEAD].astype(F32)
        for t in range(steps)
        for g in range(GROUP)
    ]
    return jnp.concatenate(pieces, axis=0).astype(BF16)


def scores_of(rows, keys):
    return lax.dot_general(rows, keys, (((1,), (1,)), ((), ())), preferred_element_type=F32)


def softmax_terms(scores):
    top = jnp.max(scores, axis=-1, keepdims=True)
    expo = jnp.exp2((scores - top) * EXPONENT_SCALE)
    return top, expo, jnp.sum(expo, axis=-1, keepdims=True)


def tail_block(rows, keys, values, slots):
    count, length = keys.shape[0], keys.shape[1]
    scores = scores_of(rows, keys.reshape(count * length, HEAD))
    scores = scores.reshape(-1, count, count * length)
    picked = scores[:, :, :length]
    for j in range(1, count):
        picked = jnp.where((slots == j)[None], scores[:, :, j * length : (j + 1) * length], picked)
    top, expo, total = softmax_terms(picked)
    spread = jnp.concatenate(
        [jnp.where((slots == j)[None], expo, 0.0) for j in range(count)], axis=-1
    )
    spread = spread.reshape(-1, count * length).astype(BF16)
    out = jnp.dot(spread, values.reshape(count * length, HEAD), preferred_element_type=F32)
    return out.reshape(-1, count, HEAD), top, total


def pack_columns(columns, first, steps, count):
    lanes = lax.broadcasted_iota(jnp.int32, (count, 128), 1)
    packed = []
    for t in range(steps):
        held = jnp.zeros((count, 128), columns.dtype)
        for g in range(GROUP):
            held = jnp.where(lanes == first + g, columns[t * GROUP + g], held)
        packed.append(held)
    return packed


def local_kernel(length, ancestors_ref, query_ref, prefix_ref, tail_ref, fresh_ref, out_ref, log_ref):
    steps, count = query_ref.shape[0], query_ref.shape[1]
    heads = prefix_ref.shape[2] // HEAD
    me = lax.axis_index("particle")
    slots = slots_on(ancestors_ref, me, me, length, count)
    own = (slots >= 0)[None]
    logs = [jnp.zeros((count, 128), F32) for _ in range(steps)]
    for k in range(heads):
        cols = slice(k * HEAD, (k + 1) * HEAD)
        rows = head_rows(query_ref, k * GROUP * HEAD)
        many = rows.shape[0]
        top1, expo1, total1 = softmax_terms(scores_of(rows, prefix_ref[0, :, cols]))
        out1 = jnp.dot(expo1.astype(BF16), prefix_ref[1, :, cols], preferred_element_type=F32)
        fresh_keys = jnp.concatenate([fresh_ref[0, s, :, cols].astype(F32) for s in range(steps)], axis=0)
        fresh_values = jnp.concatenate([fresh_ref[1, s, :, cols].astype(F32) for s in range(steps)], axis=0)
        scores2 = scores_of(rows, fresh_keys.astype(BF16))
        row = lax.broadcasted_iota(jnp.int32, scores2.shape, 0)
        col = lax.broadcasted_iota(jnp.int32, scores2.shape, 1)
        seen = (row % count == col % count) & (col // count <= row // (GROUP * count))
        top2, expo2, total2 = softmax_terms(jnp.where(seen, scores2, NEG_FILL))
        out2 = jnp.dot(expo2.astype(BF16), fresh_values.astype(BF16), preferred_element_type=F32)
        out3, top3, total3 = tail_block(rows, tail_ref[0, :, :, cols], tail_ref[1, :, :, cols], slots)
        shape = (many // count, count, 1)
        top1, total1 = top1.reshape(shape), total1.reshape(shape)
        top2, total2 = top2.reshape(shape), total2.reshape(shape)
        out1 = out1.reshape(many // count, count, HEAD)
        out2 = out2.reshape(many // count, count, HEAD)
        top3 = jnp.where(own, top3, NEG_FILL)
        top = jnp.maximum(jnp.maximum(top1, top2), top3)
        share1 = jnp.exp2((top1 - top) * EXPONENT_SCALE)
        share2 = jnp.exp2((top2 - top) * EXPONENT_SCALE)
        share3 = jnp.where(own, jnp.exp2((top3 - top) * EXPONENT_SCALE), 0.0)
        total = share1 * total1 + share2 * total2 + share3 * total3
        context = (share1 * out1 + share2 * out2 + share3 * out3) / total
        for t in range(steps):
            for g in range(GROUP):
                at = (k * GROUP + g) * HEAD
                out_ref[t, :, at : at + HEAD] = context[t * GROUP + g]
        level = top * EXPONENT_SCALE + jnp.log2(total)
        logs = [a + b for a, b in zip(logs, pack_columns(level, k * GROUP, steps, count))]
    for t in range(steps):
        log_ref[t] = logs[t]


def serve_kernel(length, reach, parity, ancestors_ref, query_ref, tail_ref, out_ref):
    steps, count = query_ref.shape[0], query_ref.shape[1]
    heads = tail_ref.shape[3] // HEAD
    lanes = heads * GROUP
    me = lax.axis_index("particle")
    slots = slots_on(ancestors_ref, partner_of(me, reach, parity), me, length, count)
    notes = [jnp.zeros((count, 128), F32) for _ in range(steps)]
    for k in range(heads):
        cols = slice(k * HEAD, (k + 1) * HEAD)
        rows = head_rows(query_ref, k * GROUP * HEAD)
        out, top, total = tail_block(rows, tail_ref[0, :, :, cols], tail_ref[1, :, :, cols], slots)
        mean = out / total
        largest = jnp.maximum(jnp.max(jnp.abs(mean), axis=-1, keepdims=True), TINY)
        power = jnp.ceil(jnp.log2(largest * (1.0 / TOP_CODE)))
        code = jnp.round(mean * jnp.exp2(-power)).astype(jnp.int32)
        for t in range(steps):
            for g in range(GROUP):
                at = (k * GROUP + g) * HEAD
                out_ref[t, :, at : at + HEAD] = code[t * GROUP + g].astype(jnp.int16)
        level = (top * EXPONENT_SCALE + jnp.log2(total)) * LOG_STEPS
        whole = jnp.round(level)
        part = jnp.round((level - whole) * LOG_FRACTION)
        for base, column in ((0, whole), (lanes, part), (2 * lanes, power)):
            packed = pack_columns(column, base + k * GROUP, steps, count)
            notes = [a + b for a, b in zip(notes, packed)]
    at = lanes * HEAD
    for t in range(steps):
        out_ref[t, :, at : at + 128] = notes[t].astype(jnp.int32).astype(jnp.int16)


def combine_kernel(length, plans, ancestors_ref, local_ref, log_ref, readout_ref, *refs):
    remote_refs, (out_ref, twist_ref) = refs[: len(plans)], refs[len(plans) :]
    steps, count = local_ref.shape[0], local_ref.shape[1]
    lanes = local_ref.shape[2] // HEAD
    me = lax.axis_index("particle")
    from_plan = [
        slots_on(ancestors_ref, me, partner_of(me, reach, parity), length, count) >= 0
        for reach, parity in plans
    ]
    away = functools.reduce(jnp.logical_or, from_plan)

    def chosen(t, at):
        value = remote_refs[0][t, :, at : at + HEAD].astype(jnp.int32)
        for ref, mine in zip(remote_refs[1:], from_plan[1:]):
            value = jnp.where(mine, ref[t, :, at : at + HEAD].astype(jnp.int32), value)
        return value.astype(F32)

    row = lax.broadcasted_iota(jnp.int32, (count, 128), 0)
    lane = lax.broadcasted_iota(jnp.int32, (count, 128), 1)
    for t in range(steps):
        notes = chosen(t, lanes * HEAD)
        whole, part, power = (notes[:, i * lanes : (i + 1) * lanes] for i in range(3))
        remote_level = (whole + part * (1.0 / LOG_FRACTION)) * (1.0 / LOG_STEPS)
        remote_level = jnp.where(away, remote_level, NEG_FILL)
        local_level = log_ref[t, :, :lanes]
        level = jnp.maximum(local_level, remote_level)
        local_share = jnp.exp2(local_level - level)
        remote_share = jnp.where(away, jnp.exp2(remote_level - level), 0.0)
        total = local_share + remote_share
        local_share = local_share / total
        remote_share = remote_share / total * jnp.exp2(power)
        gathered = jnp.zeros((count, HEAD), F32)
        for h in range(lanes):
            at = h * HEAD
            context = local_share[:, h : h + 1] * local_ref[t, :, at : at + HEAD]
            context = context + remote_share[:, h : h + 1] * chosen(t, at)
            out_ref[t, :, at : at + HEAD] = context.astype(BF16)
            gathered = gathered + context * readout_ref[:, at : at + HEAD]
        column = jnp.sum(gathered, axis=-1, keepdims=True)
        line = jnp.sum(jnp.where(row == lane, column, 0.0), axis=0, keepdims=True)
        twist_ref[t : t + 1, :] = line[:, :count]


def call(kernel, outs, name, operands, flops, limit=24 << 20):
    moved = sum(math.prod(o.shape) * o.dtype.itemsize for o in operands)
    moved += sum(math.prod(o.shape) * o.dtype.itemsize for o in outs)
    specs = [pl.BlockSpec(memory_space=SMEM)] + [pl.BlockSpec(memory_space=VMEM)] * (len(operands) - 1)
    return pl.pallas_call(
        kernel,
        out_shape=tuple(outs),
        in_specs=specs,
        out_specs=tuple(pl.BlockSpec(memory_space=VMEM) for _ in outs),
        compiler_params=pltpu.CompilerParams(vmem_limit_bytes=limit),
        cost_estimate=pl.CostEstimate(flops=flops, bytes_accessed=moved, transcendentals=0),
        name=name,
    )(*operands)


def on_device(
    length,
    prefix_cache,
    tail_cache,
    ancestors,
    queries,
    fresh_kv,
    prompt_ids,
    sampled_ids,
    twist_table,
    readout,
):
    steps, count, width = queries.shape
    lanes = width // HEAD
    plans = exchanges(length)
    asked = [lax.ppermute(queries, "particle", pairs) for _, _, pairs in plans]
    work = 4 * steps * count * width * HEAD
    tail_work = 4 * steps * count * width * count * tail_cache.shape[2]
    local_work = 4 * steps * count * width * (prefix_cache.shape[1] + count * tail_cache.shape[2]) + work
    local, logs = call(
        functools.partial(local_kernel, length),
        [
            jax.ShapeDtypeStruct(queries.shape, F32),
            jax.ShapeDtypeStruct((steps, count, 128), F32),
        ],
        "local",
        [ancestors, queries, prefix_cache, tail_cache, fresh_kv],
        local_work,
    )
    answers = []
    for (reach, parity, pairs), question in zip(plans, asked):
        (answer,) = call(
            functools.partial(serve_kernel, length, reach, parity),
            [jax.ShapeDtypeStruct((steps, count, width + 128), jnp.int16)],
            "serve",
            [ancestors, question, tail_cache],
            tail_work,
        )
        answers.append(lax.ppermute(answer, "particle", pairs))
    attended, partial_value = call(
        functools.partial(combine_kernel, length, [plan[:2] for plan in plans]),
        [
            jax.ShapeDtypeStruct(queries.shape, BF16),
            jax.ShapeDtypeStruct((steps, count), F32),
        ],
        "combine",
        [ancestors, local, logs, readout.reshape(1, width)] + answers,
        16 * steps * count * width,
    )
    other = lax.axis_size("tensor")
    swap = [(i, (i + 1) % other) for i in range(other)]
    twist_attn = partial_value + lax.ppermute(partial_value, "tensor", swap)
    repeats = jnp.sum(
        (sampled_ids[:, :, None] == prompt_ids[None, None, :]).astype(jnp.int32), axis=-1
    )
    twists = jnp.take(twist_table, sampled_ids) - 2.0 * repeats.astype(F32) + twist_attn
    return (attended, twists)


def solution(mesh):
    return jax.shard_map(
        functools.partial(on_device, mesh.shape["particle"]),
        mesh=mesh,
        in_specs=(
            P(None, "groups", "tensor"),
            P(None, ("groups", "particle"), None, "tensor"),
            P("groups"),
            P(None, ("groups", "particle"), "tensor"),
            P(None, None, ("groups", "particle"), "tensor"),
            P("groups"),
            P(None, ("groups", "particle")),
            P(),
            P("tensor"),
        ),
        out_specs=(P(None, ("groups", "particle"), "tensor"), P(None, ("groups", "particle"))),
        check_vma=False,
    )
```

```python
import functools
import math

import jax
import jax.numpy as jnp
from jax import lax
from jax.experimental import pallas as pl
from jax.experimental.pallas import tpu as pltpu
from jax.sharding import PartitionSpec as P

HEADS = 64
KV_HEADS = 8
HEAD = 128
REACH = 2
GROUP = HEADS // KV_HEADS
EXPONENT_SCALE = math.log2(math.e) / math.sqrt(HEAD)

NEG_FILL = -1e30
LOG_STEPS = 32.0
LOG_FRACTION = 65534.0
TOP_CODE = 32000.0
TINY = 1e-30

F32 = jnp.float32
BF16 = jnp.bfloat16
VMEM = pltpu.MemorySpace.VMEM
SMEM = pltpu.MemorySpace.SMEM


def exchanges(length, cores):
    found = []
    for reach in range(REACH, 0, -1):
        for parity in (0, 1):
            partner = list(range(length))
            for i in range(length - reach):
                if (i // reach) % 2 == parity:
                    partner[i], partner[i + reach] = i + reach, i
            pairs = []
            for i, other in enumerate(partner):
                turn = 1 if other == i else 0
                pairs += [(i * cores + c, other * cores + (c + turn) % cores) for c in range(cores)]
            found.append((reach, parity, pairs))
    return found


def partner_of(index, reach, parity):
    return jnp.where((index // reach) % 2 == parity, index + reach, index - reach)


def slots_on(ancestors_ref, owner, holder, length, count):
    safe = jnp.clip(owner, 0, length - 1)
    exists = safe == owner
    rows = lax.broadcasted_iota(jnp.int32, (count, 1), 0)
    slots = jnp.full((count, 1), -1, jnp.int32)
    for p in range(count):
        slot = ancestors_ref[safe * count + p] - holder * count
        here = exists & (slot >= 0) & (slot < count)
        slots = jnp.where(rows == p, jnp.where(here, slot, -1), slots)
    return slots


def head_rows(query_ref, base):
    steps = query_ref.shape[0]
    pieces = [
        query_ref[t, :, base + g * HEAD : base + (g + 1) * HEAD].astype(F32)
        for t in range(steps)
        for g in range(GROUP)
    ]
    return jnp.concatenate(pieces, axis=0).astype(BF16)


def scores_of(rows, keys):
    return lax.dot_general(rows, keys, (((1,), (1,)), ((), ())), preferred_element_type=F32)


def softmax_terms(scores):
    top = jnp.max(scores, axis=-1, keepdims=True)
    expo = jnp.exp2((scores - top) * EXPONENT_SCALE)
    return top, expo, jnp.sum(expo, axis=-1, keepdims=True)


def tail_block(rows, keys, values, slots):
    count, length = keys.shape[0], keys.shape[1]
    scores = scores_of(rows, keys.reshape(count * length, HEAD))
    scores = scores.reshape(-1, count, count * length)
    picked = scores[:, :, :length]
    for j in range(1, count):
        picked = jnp.where((slots == j)[None], scores[:, :, j * length : (j + 1) * length], picked)
    top, expo, total = softmax_terms(picked)
    spread = jnp.concatenate(
        [jnp.where((slots == j)[None], expo, 0.0) for j in range(count)], axis=-1
    )
    spread = spread.reshape(-1, count * length).astype(BF16)
    out = jnp.dot(spread, values.reshape(count * length, HEAD), preferred_element_type=F32)
    return out.reshape(-1, count, HEAD), top, total


def pack_columns(columns, first, steps, count):
    lanes = lax.broadcasted_iota(jnp.int32, (count, 128), 1)
    packed = []
    for t in range(steps):
        held = jnp.zeros((count, 128), columns.dtype)
        for g in range(GROUP):
            held = jnp.where(lanes == first + g, columns[t * GROUP + g], held)
        packed.append(held)
    return packed


def local_kernel(length, ancestors_ref, query_ref, prefix_ref, tail_ref, fresh_ref, out_ref, log_ref):
    steps, count = query_ref.shape[0], query_ref.shape[1]
    heads = prefix_ref.shape[2] // HEAD
    me = lax.axis_index("particle")
    slots = slots_on(ancestors_ref, me, me, length, count)
    own = (slots >= 0)[None]
    logs = [jnp.zeros((count, 128), F32) for _ in range(steps)]
    for k in range(heads):
        cols = slice(k * HEAD, (k + 1) * HEAD)
        rows = head_rows(query_ref, k * GROUP * HEAD)
        many = rows.shape[0]
        top1, expo1, total1 = softmax_terms(scores_of(rows, prefix_ref[0, :, cols]))
        out1 = jnp.dot(expo1.astype(BF16), prefix_ref[1, :, cols], preferred_element_type=F32)
        fresh_keys = jnp.concatenate([fresh_ref[0, s, :, cols].astype(F32) for s in range(steps)], axis=0)
        fresh_values = jnp.concatenate([fresh_ref[1, s, :, cols].astype(F32) for s in range(steps)], axis=0)
        scores2 = scores_of(rows, fresh_keys.astype(BF16))
        row = lax.broadcasted_iota(jnp.int32, scores2.shape, 0)
        col = lax.broadcasted_iota(jnp.int32, scores2.shape, 1)
        seen = (row % count == col % count) & (col // count <= row // (GROUP * count))
        top2, expo2, total2 = softmax_terms(jnp.where(seen, scores2, NEG_FILL))
        out2 = jnp.dot(expo2.astype(BF16), fresh_values.astype(BF16), preferred_element_type=F32)
        out3, top3, total3 = tail_block(rows, tail_ref[0, :, :, cols], tail_ref[1, :, :, cols], slots)
        shape = (many // count, count, 1)
        top1, total1 = top1.reshape(shape), total1.reshape(shape)
        top2, total2 = top2.reshape(shape), total2.reshape(shape)
        out1 = out1.reshape(many // count, count, HEAD)
        out2 = out2.reshape(many // count, count, HEAD)
        top3 = jnp.where(own, top3, NEG_FILL)
        top = jnp.maximum(jnp.maximum(top1, top2), top3)
        share1 = jnp.exp2((top1 - top) * EXPONENT_SCALE)
        share2 = jnp.exp2((top2 - top) * EXPONENT_SCALE)
        share3 = jnp.where(own, jnp.exp2((top3 - top) * EXPONENT_SCALE), 0.0)
        total = share1 * total1 + share2 * total2 + share3 * total3
        context = (share1 * out1 + share2 * out2 + share3 * out3) / total
        for t in range(steps):
            for g in range(GROUP):
                at = (k * GROUP + g) * HEAD
                out_ref[t, :, at : at + HEAD] = context[t * GROUP + g]
        level = top * EXPONENT_SCALE + jnp.log2(total)
        logs = [a + b for a, b in zip(logs, pack_columns(level, k * GROUP, steps, count))]
    for t in range(steps):
        log_ref[t] = logs[t]


def serve_kernel(length, reach, parity, ancestors_ref, query_ref, tail_ref, out_ref):
    steps, count = query_ref.shape[0], query_ref.shape[1]
    heads = tail_ref.shape[3] // HEAD
    lanes = heads * GROUP
    me = lax.axis_index("particle")
    slots = slots_on(ancestors_ref, partner_of(me, reach, parity), me, length, count)
    notes = [jnp.zeros((count, 128), F32) for _ in range(steps)]
    for k in range(heads):
        cols = slice(k * HEAD, (k + 1) * HEAD)
        rows = head_rows(query_ref, k * GROUP * HEAD)
        out, top, total = tail_block(rows, tail_ref[0, :, :, cols], tail_ref[1, :, :, cols], slots)
        mean = out / total
        largest = jnp.maximum(jnp.max(jnp.abs(mean), axis=-1, keepdims=True), TINY)
        power = jnp.ceil(jnp.log2(largest * (1.0 / TOP_CODE)))
        code = jnp.round(mean * jnp.exp2(-power)).astype(jnp.int32)
        for t in range(steps):
            for g in range(GROUP):
                at = (k * GROUP + g) * HEAD
                out_ref[t, :, at : at + HEAD] = code[t * GROUP + g].astype(jnp.int16)
        level = (top * EXPONENT_SCALE + jnp.log2(total)) * LOG_STEPS
        whole = jnp.round(level)
        part = jnp.round((level - whole) * LOG_FRACTION)
        for base, column in ((0, whole), (lanes, part), (2 * lanes, power)):
            packed = pack_columns(column, base + k * GROUP, steps, count)
            notes = [a + b for a, b in zip(notes, packed)]
    at = lanes * HEAD
    for t in range(steps):
        out_ref[t, :, at : at + 128] = notes[t].astype(jnp.int32).astype(jnp.int16)


def combine_kernel(length, plans, ancestors_ref, local_ref, log_ref, readout_ref, *refs):
    remote_refs, (out_ref, twist_ref) = refs[: len(plans)], refs[len(plans) :]
    steps, count = local_ref.shape[0], local_ref.shape[1]
    lanes = local_ref.shape[2] // HEAD
    me = lax.axis_index("particle")
    from_plan = [
        slots_on(ancestors_ref, me, partner_of(me, reach, parity), length, count) >= 0
        for reach, parity in plans
    ]
    away = functools.reduce(jnp.logical_or, from_plan)

    def chosen(t, at):
        value = remote_refs[0][t, :, at : at + HEAD].astype(jnp.int32)
        for ref, mine in zip(remote_refs[1:], from_plan[1:]):
            value = jnp.where(mine, ref[t, :, at : at + HEAD].astype(jnp.int32), value)
        return value.astype(F32)

    row = lax.broadcasted_iota(jnp.int32, (count, 128), 0)
    lane = lax.broadcasted_iota(jnp.int32, (count, 128), 1)
    for t in range(steps):
        notes = chosen(t, lanes * HEAD)
        whole, part, power = (notes[:, i * lanes : (i + 1) * lanes] for i in range(3))
        remote_level = (whole + part * (1.0 / LOG_FRACTION)) * (1.0 / LOG_STEPS)
        remote_level = jnp.where(away, remote_level, NEG_FILL)
        local_level = log_ref[t, :, :lanes]
        level = jnp.maximum(local_level, remote_level)
        local_share = jnp.exp2(local_level - level)
        remote_share = jnp.where(away, jnp.exp2(remote_level - level), 0.0)
        total = local_share + remote_share
        local_share = local_share / total
        remote_share = remote_share / total * jnp.exp2(power)
        gathered = jnp.zeros((count, HEAD), F32)
        for h in range(lanes):
            at = h * HEAD
            context = local_share[:, h : h + 1] * local_ref[t, :, at : at + HEAD]
            context = context + remote_share[:, h : h + 1] * chosen(t, at)
            out_ref[t, :, at : at + HEAD] = context.astype(BF16)
            gathered = gathered + context * readout_ref[:, at : at + HEAD]
        column = jnp.sum(gathered, axis=-1, keepdims=True)
        line = jnp.sum(jnp.where(row == lane, column, 0.0), axis=0, keepdims=True)
        twist_ref[t : t + 1, :] = line[:, :count]


def call(kernel, outs, name, operands, flops, limit=24 << 20):
    moved = sum(math.prod(o.shape) * o.dtype.itemsize for o in operands)
    moved += sum(math.prod(o.shape) * o.dtype.itemsize for o in outs)
    specs = [pl.BlockSpec(memory_space=SMEM)] + [pl.BlockSpec(memory_space=VMEM)] * (len(operands) - 1)
    return pl.pallas_call(
        kernel,
        out_shape=tuple(outs),
        in_specs=specs,
        out_specs=tuple(pl.BlockSpec(memory_space=VMEM) for _ in outs),
        compiler_params=pltpu.CompilerParams(vmem_limit_bytes=limit),
        cost_estimate=pl.CostEstimate(flops=flops, bytes_accessed=moved, transcendentals=0),
        name=name,
    )(*operands)


def on_device(
    length,
    prefix_cache,
    tail_cache,
    ancestors,
    queries,
    fresh_kv,
    prompt_ids,
    sampled_ids,
    twist_table,
    readout,
):
    steps, count, width = queries.shape
    lanes = width // HEAD
    cores = lax.axis_size("tensor")
    plans = exchanges(length, cores)
    asked = [lax.ppermute(queries, ("particle", "tensor"), pairs) for _, _, pairs in plans]
    work = 4 * steps * count * width * HEAD
    tail_work = 4 * steps * count * width * count * tail_cache.shape[2]
    local_work = 4 * steps * count * width * (prefix_cache.shape[1] + count * tail_cache.shape[2]) + work
    local, logs = call(
        functools.partial(local_kernel, length),
        [
            jax.ShapeDtypeStruct(queries.shape, F32),
            jax.ShapeDtypeStruct((steps, count, 128), F32),
        ],
        "local",
        [ancestors, queries, prefix_cache, tail_cache, fresh_kv],
        local_work,
    )
    answers = []
    for (reach, parity, pairs), question in zip(plans, asked):
        (answer,) = call(
            functools.partial(serve_kernel, length, reach, parity),
            [jax.ShapeDtypeStruct((steps, count, width + 128), jnp.int16)],
            "serve",
            [ancestors, question, tail_cache],
            tail_work,
        )
        answers.append(lax.ppermute(answer, ("particle", "tensor"), pairs))
    attended, partial_value = call(
        functools.partial(combine_kernel, length, [plan[:2] for plan in plans]),
        [
            jax.ShapeDtypeStruct(queries.shape, BF16),
            jax.ShapeDtypeStruct((steps, count), F32),
        ],
        "combine",
        [ancestors, local, logs, readout.reshape(1, width)] + answers,
        16 * steps * count * width,
    )
    if cores == 2:
        twist_attn = partial_value + lax.ppermute(partial_value, "tensor", [(0, 1), (1, 0)])
    else:
        twist_attn = lax.psum(partial_value, "tensor")
    repeats = jnp.sum(
        (sampled_ids[:, :, None] == prompt_ids[None, None, :]).astype(jnp.int32), axis=-1
    )
    twists = twist_table.at[sampled_ids].get(mode="promise_in_bounds") - 2.0 * repeats.astype(F32) + twist_attn
    return (attended, twists)


def solution(mesh):
    return jax.shard_map(
        functools.partial(on_device, mesh.shape["particle"]),
        mesh=mesh,
        in_specs=(
            P(None, "groups", "tensor"),
            P(None, ("groups", "particle"), None, "tensor"),
            P("groups"),
            P(None, ("groups", "particle"), "tensor"),
            P(None, None, ("groups", "particle"), "tensor"),
            P("groups"),
            P(None, ("groups", "particle")),
            P(),
            P("tensor"),
        ),
        out_specs=(P(None, ("groups", "particle"), "tensor"), P(None, ("groups", "particle"))),
        check_vma=False,
    )
```

```python
import functools
import math

import jax
import jax.numpy as jnp
from jax import lax
from jax.experimental import pallas as pl
from jax.experimental.pallas import tpu as pltpu
from jax.sharding import PartitionSpec as P

HEADS = 64
KV_HEADS = 8
HEAD = 128
REACH = 2
GROUP = HEADS // KV_HEADS
EXPONENT_SCALE = math.log2(math.e) / math.sqrt(HEAD)

NEG_FILL = -1e30
LOG_STEPS = 32.0
LOG_FRACTION = 65534.0
TOP_CODE = 32000.0
TINY = 1e-30
LANES = 128

F32 = jnp.float32
BF16 = jnp.bfloat16
VMEM = pltpu.MemorySpace.VMEM
SMEM = pltpu.MemorySpace.SMEM


def exchanges(length, cores):
    found = []
    for reach in range(REACH, 0, -1):
        for parity in (0, 1):
            partner = list(range(length))
            for i in range(length - reach):
                if (i // reach) % 2 == parity:
                    partner[i], partner[i + reach] = i + reach, i
            pairs = []
            for i, other in enumerate(partner):
                turn = 1 if other == i else 0
                pairs += [(i * cores + c, other * cores + (c + turn) % cores) for c in range(cores)]
            found.append((reach, parity, pairs))
    return found


def partner_of(index, reach, parity):
    return jnp.where((index // reach) % 2 == parity, index + reach, index - reach)


def held_by(ancestors_ref, owner, holder, length, count):
    safe = jnp.clip(owner, 0, length - 1)
    exists = safe == owner
    found = []
    for p in range(count):
        slot = ancestors_ref[safe * count + p] - holder * count
        found.append((exists & (slot >= 0) & (slot < count), jnp.clip(slot, 0, count - 1)))
    return found


def head_tiles(query_ref, base):
    return [
        query_ref[t, :, base + g * HEAD : base + (g + 1) * HEAD].astype(F32)
        for t in range(query_ref.shape[0])
        for g in range(GROUP)
    ]


def scores_of(rows, keys):
    return lax.dot_general(rows, keys, (((1,), (1,)), ((), ())), preferred_element_type=F32)


def softmax_terms(scores):
    top = jnp.max(scores, axis=-1, keepdims=True)
    expo = jnp.exp2((scores - top) * EXPONENT_SCALE)
    return top, expo, jnp.sum(expo, axis=-1, keepdims=True)


def two_codes(value):
    value = value * LOG_STEPS
    whole = jnp.round(value)
    return whole, jnp.round((value - whole) * LOG_FRACTION)


def from_codes(whole, part):
    return (whole + part * (1.0 / LOG_FRACTION)) * (1.0 / LOG_STEPS)


def serve(slots, query_ref, tail_ref, out_ref):
    steps, count = query_ref.shape[0], query_ref.shape[1]
    heads = tail_ref.shape[3] // HEAD
    many = steps * GROUP
    each = heads * many
    lane = lax.broadcasted_iota(jnp.int32, (GROUP, LANES), 1)
    row = lax.broadcasted_iota(jnp.int32, (GROUP, LANES), 0)
    notes = [[jnp.zeros((GROUP, LANES), F32) for _ in range(count)] for _ in range(3)]
    scores = []
    for k in range(heads):
        tiles = jnp.stack(head_tiles(query_ref, k * GROUP * HEAD), axis=0)
        rows = jnp.swapaxes(tiles, 0, 1).astype(BF16)
        cols = slice(k * HEAD, (k + 1) * HEAD)
        scores += [scores_of(rows[p], tail_ref[0, slots[p], :, cols]) for p in range(count)]
    terms = [softmax_terms(score) for score in scores]
    outs = [
        jnp.dot(
            terms[k * count + p][1].astype(BF16),
            tail_ref[1, slots[p], :, k * HEAD : (k + 1) * HEAD],
            preferred_element_type=F32,
        )
        for k in range(heads)
        for p in range(count)
    ]
    for k in range(heads):
        for p in range(count):
            top, _, total = terms[k * count + p]
            out = outs[k * count + p]
            largest = jnp.maximum(jnp.max(jnp.abs(out), axis=-1, keepdims=True), TINY)
            code = jnp.round(out * (TOP_CODE / largest)).astype(jnp.int32)
            at = p * each + k * many
            out_ref[at : at + many, :] = code.astype(jnp.int16)
            for t in range(steps):
                here = lane == row + (k * many + t * GROUP)
                part = slice(t * GROUP, (t + 1) * GROUP)
                for note, column in zip(notes, (top, total, largest)):
                    note[p] = jnp.where(here, column[part], note[p])
    top, total, largest = (
        jnp.concatenate([jnp.sum(n, axis=0, keepdims=True) for n in note], axis=0) for note in notes
    )
    if each < LANES:
        total, largest = jnp.maximum(total, TINY), jnp.maximum(largest, TINY)
    spread = jnp.log2(total)
    level = two_codes(top * EXPONENT_SCALE + spread)
    scale = two_codes(jnp.log2(largest) - spread - math.log2(TOP_CODE))
    coded = jnp.concatenate(level + scale, axis=0).astype(jnp.int32)
    out_ref[count * each :, :] = coded.astype(jnp.int16)


def serve_kernel(length, reach, parity, ancestors_ref, query_ref, tail_ref, out_ref):
    count = query_ref.shape[1]
    me = lax.axis_index("particle")
    found = held_by(ancestors_ref, partner_of(me, reach, parity), me, length, count)
    serve([slot for _, slot in found], query_ref, tail_ref, out_ref)


def serve_own_kernel(length, ancestors_ref, query_ref, tail_ref, out_ref, held_ref, sem):
    copy = pltpu.make_async_copy(tail_ref, held_ref, sem)
    copy.start()
    count = query_ref.shape[1]
    me = lax.axis_index("particle")
    found = held_by(ancestors_ref, me, me, length, count)
    copy.wait()
    serve([slot for _, slot in found], query_ref, held_ref, out_ref)


def local_kernel(query_ref, prefix_ref, fresh_ref, out_ref, log_ref):
    steps, count = query_ref.shape[0], query_ref.shape[1]
    heads = prefix_ref.shape[2] // HEAD
    many = steps * GROUP
    lane = lax.broadcasted_iota(jnp.int32, (count, LANES), 1)
    logs = []
    for k in range(heads):
        cols = slice(k * HEAD, (k + 1) * HEAD)
        rows = jnp.concatenate(head_tiles(query_ref, k * GROUP * HEAD), axis=0).astype(BF16)
        top1, expo1, total1 = softmax_terms(scores_of(rows, prefix_ref[0, :, cols]))
        out1 = jnp.dot(expo1.astype(BF16), prefix_ref[1, :, cols], preferred_element_type=F32)
        fresh_keys = jnp.concatenate([fresh_ref[0, s, :, cols].astype(F32) for s in range(steps)], axis=0)
        fresh_values = jnp.concatenate([fresh_ref[1, s, :, cols].astype(F32) for s in range(steps)], axis=0)
        scores2 = scores_of(rows, fresh_keys.astype(BF16))
        row = lax.broadcasted_iota(jnp.int32, scores2.shape, 0)
        col = lax.broadcasted_iota(jnp.int32, scores2.shape, 1)
        seen = (row % count == col % count) & (col // count <= row // (GROUP * count))
        top2, expo2, total2 = softmax_terms(jnp.where(seen, scores2, NEG_FILL))
        out2 = jnp.dot(expo2.astype(BF16), fresh_values.astype(BF16), preferred_element_type=F32)
        top = jnp.maximum(top1, top2)
        share1 = jnp.exp2((top1 - top) * EXPONENT_SCALE)
        share2 = jnp.exp2((top2 - top) * EXPONENT_SCALE)
        total = share1 * total1 + share2 * total2
        context = (share1 * out1 + share2 * out2) / total
        context = context.reshape(many, count, HEAD)
        top, total = top.reshape(many, count, 1), total.reshape(many, count, 1)
        held = [jnp.zeros((count, LANES), F32) for _ in range(2)]
        for t in range(steps):
            for g in range(GROUP):
                at = (k * GROUP + g) * HEAD
                r = t * GROUP + g
                out_ref[t, :, at : at + HEAD] = context[r]
                held[0] = jnp.where(lane == k * many + r, top[r], held[0])
                held[1] = jnp.where(lane == k * many + r, total[r], held[1])
        inside = (lane >= k * many) & (lane < (k + 1) * many)
        level = held[0] * EXPONENT_SCALE + jnp.log2(jnp.where(inside, held[1], 1.0))
        logs.append(level)
    log_ref[...] = functools.reduce(jnp.add, logs)


def combine_kernel(length, plans, ancestors_ref, local_ref, log_ref, readout_ref, *refs):
    sent_refs, (out_ref, twist_ref) = refs[: len(plans) + 1], refs[len(plans) + 1 :]
    steps, count = local_ref.shape[0], local_ref.shape[1]
    heads = local_ref.shape[2] // (HEAD * GROUP)
    many = steps * GROUP
    each = heads * many
    me = lax.axis_index("particle")
    source = [jnp.int32(0)] * count
    for m, (reach, parity) in enumerate(plans):
        found = held_by(ancestors_ref, me, partner_of(me, reach, parity), length, count)
        source = [jnp.where(here, m + 1, old) for (here, _), old in zip(found, source)]
    row = lax.broadcasted_iota(jnp.int32, (count, LANES), 0)
    lane = lax.broadcasted_iota(jnp.int32, (count, LANES), 1)

    def notes_of(ref):
        notes = ref[count * each :, :].astype(jnp.int32).astype(F32)
        return [notes[i * count : (i + 1) * count] for i in range(4)]

    sources = jnp.zeros((count, LANES), jnp.int32)
    for p in range(count):
        sources = jnp.where(row == p, source[p], sources)
    notes = notes_of(sent_refs[0])
    for m, ref in enumerate(sent_refs[1:], 1):
        notes = [jnp.where(sources == m, new, old) for new, old in zip(notes_of(ref), notes)]
    remote_level, scale = from_codes(*notes[:2]), from_codes(*notes[2:])
    local_level = log_ref[...]
    level = jnp.maximum(local_level, remote_level)
    local_share = jnp.exp2(local_level - level)
    remote_share = jnp.exp2(remote_level - level)
    total = local_share + remote_share
    local_share = local_share / total
    remote_share = remote_share / total * jnp.exp2(scale)
    gathered = [jnp.zeros((count, HEAD), F32) for _ in range(steps)]
    for k in range(heads):
        for pair in range(steps // 2):
            at = k * many + pair * 2 * GROUP
            picked = []
            for p in range(count):
                here = slice(p * each + at, p * each + at + 2 * GROUP)
                code = sent_refs[0][here, :]
                for m, ref in enumerate(sent_refs[1:], 1):
                    code = jnp.where(source[p] == m, ref[here, :], code)
                picked.append(code.astype(jnp.int32).astype(F32))
            tiles = jnp.swapaxes(jnp.stack(picked, axis=0), 0, 1)
            for r in range(2 * GROUP):
                t, h = pair * 2 + r // GROUP, k * GROUP + r % GROUP
                cols = slice(h * HEAD, (h + 1) * HEAD)
                context = local_share[:, at + r : at + r + 1] * local_ref[t, :, cols]
                context = context + remote_share[:, at + r : at + r + 1] * tiles[r]
                out_ref[t, :, cols] = context.astype(BF16)
                gathered[t] = gathered[t] + context * readout_ref[:, cols]
    for t in range(steps):
        column = jnp.sum(gathered[t], axis=-1, keepdims=True)
        line = jnp.sum(jnp.where(row == lane, column, 0.0), axis=0, keepdims=True)
        twist_ref[t : t + 1, :] = line[:, :count]


def call(kernel, outs, name, operands, flops, spaces=None, scratch=(), limit=24 << 20):
    moved = sum(math.prod(o.shape) * o.dtype.itemsize for o in operands)
    moved += sum(math.prod(o.shape) * o.dtype.itemsize for o in outs)
    spaces = spaces or [SMEM] + [VMEM] * (len(operands) - 1)
    return pl.pallas_call(
        kernel,
        out_shape=tuple(outs),
        in_specs=[pl.BlockSpec(memory_space=space) for space in spaces],
        out_specs=tuple(pl.BlockSpec(memory_space=VMEM) for _ in outs),
        scratch_shapes=scratch,
        compiler_params=pltpu.CompilerParams(vmem_limit_bytes=limit),
        cost_estimate=pl.CostEstimate(flops=flops, bytes_accessed=moved, transcendentals=0),
        name=name,
    )(*operands)


def on_device(
    length,
    prefix_cache,
    tail_cache,
    ancestors,
    queries,
    fresh_kv,
    prompt_ids,
    sampled_ids,
    twist_table,
    readout,
):
    steps, count, width = queries.shape
    rows = steps * width // HEAD
    assert rows <= LANES and steps % 2 == 0
    cores = lax.axis_size("tensor")
    both = ("particle", "tensor")
    plans = exchanges(length, cores)
    asked = [lax.ppermute(queries, both, pairs) for _, _, pairs in plans]
    reply = jax.ShapeDtypeStruct((count * rows + 4 * count, HEAD), jnp.int16)
    tail_work = 4 * steps * count * width * tail_cache.shape[2]
    local_work = 4 * steps * count * width * prefix_cache.shape[1]
    own, tails = call(
        functools.partial(serve_own_kernel, length),
        [reply, jax.ShapeDtypeStruct(tail_cache.shape, tail_cache.dtype)],
        "own",
        [ancestors, queries, tail_cache],
        tail_work,
        spaces=[SMEM, VMEM, pl.ANY],
        scratch=(pltpu.SemaphoreType.DMA,),
    )
    answers = [own]
    for (reach, parity, pairs), question in zip(plans, asked):
        (answer,) = call(
            functools.partial(serve_kernel, length, reach, parity),
            [reply],
            "serve",
            [ancestors, question, tails],
            tail_work,
        )
        answers.append(lax.ppermute(answer, both, pairs))
    local, logs = call(
        local_kernel,
        [jax.ShapeDtypeStruct(queries.shape, F32), jax.ShapeDtypeStruct((count, LANES), F32)],
        "local",
        [queries, prefix_cache, fresh_kv],
        local_work,
        spaces=[VMEM] * 3,
    )
    attended, partial_value = call(
        functools.partial(combine_kernel, length, [plan[:2] for plan in plans]),
        [jax.ShapeDtypeStruct(queries.shape, BF16), jax.ShapeDtypeStruct((steps, count), F32)],
        "combine",
        [ancestors, local, logs, readout.reshape(1, width)] + answers,
        16 * steps * count * width,
    )
    if cores == 2:
        twist_attn = partial_value + lax.ppermute(partial_value, "tensor", [(0, 1), (1, 0)])
    else:
        twist_attn = lax.psum(partial_value, "tensor")
    repeats = jnp.sum(
        (sampled_ids[:, :, None] == prompt_ids[None, None, :]).astype(jnp.int32), axis=-1
    )
    twists = twist_table.at[sampled_ids].get(mode="promise_in_bounds") - 2.0 * repeats.astype(F32) + twist_attn
    return (attended, twists)


def solution(mesh):
    return jax.shard_map(
        functools.partial(on_device, mesh.shape["particle"]),
        mesh=mesh,
        in_specs=(
            P(None, "groups", "tensor"),
            P(None, ("groups", "particle"), None, "tensor"),
            P("groups"),
            P(None, ("groups", "particle"), "tensor"),
            P(None, None, ("groups", "particle"), "tensor"),
            P("groups"),
            P(None, ("groups", "particle")),
            P(),
            P("tensor"),
        ),
        out_specs=(P(None, ("groups", "particle"), "tensor"), P(None, ("groups", "particle"))),
        check_vma=False,
    )
```

```python
import functools
import math

import jax
import jax.numpy as jnp
from jax import lax
from jax.experimental import pallas as pl
from jax.experimental.pallas import tpu as pltpu
from jax.sharding import PartitionSpec as P


HEADS = 64
KV_HEADS = 8
HEAD = 128
EXCHANGES = ((1, 0), (2, 0), (2, 1), (1, 1))
GROUP = HEADS // KV_HEADS
EXPONENT_SCALE = math.log2(math.e) / math.sqrt(HEAD)

NEG_FILL = -1e30
LOG_STEPS = 32.0
LOG_FRACTION = 65534.0
TOP_CODE = 32000.0
TINY = 1e-30
LANES = 128

F32 = jnp.float32
BF16 = jnp.bfloat16
VMEM = pltpu.MemorySpace.VMEM
SMEM = pltpu.MemorySpace.SMEM


def exchanges(length, cores):
    found = []
    for reach, parity in EXCHANGES:
        partner = list(range(length))
        for i in range(length - reach):
            if (i // reach) % 2 == parity:
                partner[i], partner[i + reach] = i + reach, i
        pairs = []
        for i, other in enumerate(partner):
            turn = 1 if other == i else 0
            pairs += [(i * cores + c, other * cores + (c + turn) % cores) for c in range(cores)]
        found.append((reach, parity, pairs))
    return found


def partner_of(index, reach, parity):
    return jnp.where((index // reach) % 2 == parity, index + reach, index - reach)


def held_by(ancestors_ref, owner, holder, length, count):
    safe = jnp.clip(owner, 0, length - 1)
    exists = safe == owner
    found = []
    for p in range(count):
        slot = ancestors_ref[safe * count + p] - holder * count
        found.append((exists & (slot >= 0) & (slot < count), jnp.clip(slot, 0, count - 1)))
    return found


def head_tiles(query_ref, base):
    return [
        query_ref[t, :, base + g * HEAD : base + (g + 1) * HEAD].astype(F32)
        for t in range(query_ref.shape[0])
        for g in range(GROUP)
    ]


def scores_of(rows, keys):
    return lax.dot_general(rows, keys, (((1,), (1,)), ((), ())), preferred_element_type=F32)


def softmax_terms(scores):
    top = jnp.max(scores, axis=-1, keepdims=True)
    expo = jnp.exp2((scores - top) * EXPONENT_SCALE)
    return top, expo, jnp.sum(expo, axis=-1, keepdims=True)


def two_codes(value):
    value = value * LOG_STEPS
    whole = jnp.round(value)
    return whole, jnp.round((value - whole) * LOG_FRACTION)


def from_codes(whole, part):
    return (whole + part * (1.0 / LOG_FRACTION)) * (1.0 / LOG_STEPS)


def serve(slots, query_ref, tail_ref, out_ref):
    steps, count = query_ref.shape[0], query_ref.shape[1]
    heads = tail_ref.shape[3] // HEAD
    many = steps * GROUP
    each = heads * many
    lane = lax.broadcasted_iota(jnp.int32, (GROUP, LANES), 1)
    row = lax.broadcasted_iota(jnp.int32, (GROUP, LANES), 0)
    notes = [[jnp.zeros((GROUP, LANES), F32) for _ in range(count)] for _ in range(3)]
    scores = []
    for k in range(heads):
        tiles = jnp.stack(head_tiles(query_ref, k * GROUP * HEAD), axis=0)
        rows = jnp.swapaxes(tiles, 0, 1).astype(BF16)
        cols = slice(k * HEAD, (k + 1) * HEAD)
        scores += [scores_of(rows[p], tail_ref[0, slots[p], :, cols]) for p in range(count)]
    terms = [softmax_terms(score) for score in scores]
    outs = [
        jnp.dot(
            terms[k * count + p][1].astype(BF16),
            tail_ref[1, slots[p], :, k * HEAD : (k + 1) * HEAD],
            preferred_element_type=F32,
        )
        for k in range(heads)
        for p in range(count)
    ]
    for k in range(heads):
        for p in range(count):
            top, _, total = terms[k * count + p]
            out = outs[k * count + p]
            largest = jnp.maximum(jnp.max(jnp.abs(out), axis=-1, keepdims=True), TINY)
            code = jnp.round(out * (TOP_CODE / largest)).astype(jnp.int32)
            at = p * each + k * many
            out_ref[at : at + many, :] = code.astype(jnp.int16)
            for t in range(steps):
                here = lane == row + (k * many + t * GROUP)
                part = slice(t * GROUP, (t + 1) * GROUP)
                for note, column in zip(notes, (top, total, largest)):
                    note[p] = jnp.where(here, column[part], note[p])
    top, total, largest = (
        jnp.concatenate([jnp.sum(n, axis=0, keepdims=True) for n in note], axis=0) for note in notes
    )
    if each < LANES:
        total, largest = jnp.maximum(total, TINY), jnp.maximum(largest, TINY)
    spread = jnp.log2(total)
    level = two_codes(top * EXPONENT_SCALE + spread)
    scale = two_codes(jnp.log2(largest) - spread - math.log2(TOP_CODE))
    coded = jnp.concatenate(level + scale, axis=0).astype(jnp.int32)
    out_ref[count * each :, :] = coded.astype(jnp.int16)


def serve_kernel(length, reach, parity, ancestors_ref, query_ref, tail_ref, _, out_ref):
    count = query_ref.shape[1]
    me = lax.axis_index("particle")
    found = held_by(ancestors_ref, partner_of(me, reach, parity), me, length, count)
    serve([slot for _, slot in found], query_ref, tail_ref, out_ref)


def serve_own_kernel(
    length,
    ancestors_ref,
    query_ref,
    tail_ref,
    list_ref,
    out_ref,
    held_ref,
    list_out,
    sems,
):
    copies = [
        pltpu.make_async_copy(tail_ref, held_ref, sems.at[0]),
        pltpu.make_async_copy(list_ref, list_out, sems.at[1]),
    ]
    for copy in copies:
        copy.start()
    count = query_ref.shape[1]
    me = lax.axis_index("particle")
    found = held_by(ancestors_ref, me, me, length, count)
    serve([slot for _, slot in found], query_ref, tail_ref, out_ref)
    for copy in copies:
        copy.wait()


def local_kernel(query_ref, prefix_ref, fresh_ref, out_ref, log_ref):
    steps, count = query_ref.shape[0], query_ref.shape[1]
    heads = prefix_ref.shape[2] // HEAD
    many = steps * GROUP
    lane = lax.broadcasted_iota(jnp.int32, (count, LANES), 1)
    logs = []
    for k in range(heads):
        cols = slice(k * HEAD, (k + 1) * HEAD)
        rows = jnp.concatenate(head_tiles(query_ref, k * GROUP * HEAD), axis=0).astype(BF16)
        top1, expo1, total1 = softmax_terms(scores_of(rows, prefix_ref[0, :, cols]))
        out1 = jnp.dot(expo1.astype(BF16), prefix_ref[1, :, cols], preferred_element_type=F32)
        fresh_keys = jnp.concatenate([fresh_ref[0, s, :, cols].astype(F32) for s in range(steps)], axis=0)
        fresh_values = jnp.concatenate([fresh_ref[1, s, :, cols].astype(F32) for s in range(steps)], axis=0)
        scores2 = scores_of(rows, fresh_keys.astype(BF16))
        row = lax.broadcasted_iota(jnp.int32, scores2.shape, 0)
        col = lax.broadcasted_iota(jnp.int32, scores2.shape, 1)
        seen = (row % count == col % count) & (col // count <= row // (GROUP * count))
        top2, expo2, total2 = softmax_terms(jnp.where(seen, scores2, NEG_FILL))
        out2 = jnp.dot(expo2.astype(BF16), fresh_values.astype(BF16), preferred_element_type=F32)
        top = jnp.maximum(top1, top2)
        share1 = jnp.exp2((top1 - top) * EXPONENT_SCALE)
        share2 = jnp.exp2((top2 - top) * EXPONENT_SCALE)
        total = share1 * total1 + share2 * total2
        context = (share1 * out1 + share2 * out2) / total
        context = context.reshape(many, count, HEAD)
        top, total = top.reshape(many, count, 1), total.reshape(many, count, 1)
        held = [jnp.zeros((count, LANES), F32) for _ in range(2)]
        for t in range(steps):
            for g in range(GROUP):
                at = (k * GROUP + g) * HEAD
                r = t * GROUP + g
                out_ref[t, :, at : at + HEAD] = context[r]
                held[0] = jnp.where(lane == k * many + r, top[r], held[0])
                held[1] = jnp.where(lane == k * many + r, total[r], held[1])
        inside = (lane >= k * many) & (lane < (k + 1) * many)
        level = held[0] * EXPONENT_SCALE + jnp.log2(jnp.where(inside, held[1], 1.0))
        logs.append(level)
    log_ref[...] = functools.reduce(jnp.add, logs)


def combine_kernel(length, plans, ancestors_ref, local_ref, log_ref, readout_ref, base_ref, *refs):
    sent_refs, (out_ref, twist_ref) = refs[: len(plans) + 1], refs[len(plans) + 1 :]
    steps, count = local_ref.shape[0], local_ref.shape[1]
    heads = local_ref.shape[2] // (HEAD * GROUP)
    many = steps * GROUP
    each = heads * many
    me = lax.axis_index("particle")
    source = [jnp.int32(0)] * count
    for m, (reach, parity) in enumerate(plans):
        found = held_by(ancestors_ref, me, partner_of(me, reach, parity), length, count)
        source = [jnp.where(here, m + 1, old) for (here, _), old in zip(found, source)]
    row = lax.broadcasted_iota(jnp.int32, (count, LANES), 0)
    lane = lax.broadcasted_iota(jnp.int32, (count, LANES), 1)

    def notes_of(ref):
        notes = ref[count * each :, :].astype(jnp.int32).astype(F32)
        return [notes[i * count : (i + 1) * count] for i in range(4)]

    sources = jnp.zeros((count, LANES), jnp.int32)
    for p in range(count):
        sources = jnp.where(row == p, source[p], sources)
    notes = notes_of(sent_refs[0])
    for m, ref in enumerate(sent_refs[1:], 1):
        notes = [jnp.where(sources == m, new, old) for new, old in zip(notes_of(ref), notes)]
    remote_level, scale = from_codes(*notes[:2]), from_codes(*notes[2:])
    local_level = log_ref[...]
    level = jnp.maximum(local_level, remote_level)
    local_share = jnp.exp2(local_level - level)
    remote_share = jnp.exp2(remote_level - level)
    total = local_share + remote_share
    local_share = local_share / total
    remote_share = remote_share / total * jnp.exp2(scale)
    gathered = [jnp.zeros((count, HEAD), F32) for _ in range(steps)]
    for k in range(heads):
        for pair in range(steps // 2):
            at = k * many + pair * 2 * GROUP
            picked = []
            for p in range(count):
                here = slice(p * each + at, p * each + at + 2 * GROUP)
                code = sent_refs[0][here, :]
                for m, ref in enumerate(sent_refs[1:], 1):
                    code = jnp.where(source[p] == m, ref[here, :], code)
                picked.append(code.astype(jnp.int32).astype(F32))
            tiles = jnp.swapaxes(jnp.stack(picked, axis=0), 0, 1)
            for r in range(2 * GROUP):
                t, h = pair * 2 + r // GROUP, k * GROUP + r % GROUP
                cols = slice(h * HEAD, (h + 1) * HEAD)
                context = local_share[:, at + r : at + r + 1] * local_ref[t, :, cols]
                context = context + remote_share[:, at + r : at + r + 1] * tiles[r]
                out_ref[t, :, cols] = context.astype(BF16)
                gathered[t] = gathered[t] + context * readout_ref[:, cols]
    for t in range(steps):
        column = jnp.sum(gathered[t], axis=-1, keepdims=True)
        line = jnp.sum(jnp.where(row == lane, column, 0.0), axis=0, keepdims=True)
        twist_ref[t : t + 1, :] = line[:, :count] + base_ref[t : t + 1, :]


def call(kernel, outs, operands, flops, spaces=None, scratch=(), limit=24 << 20):
    moved = sum(math.prod(o.shape) * o.dtype.itemsize for o in operands)
    moved += sum(math.prod(o.shape) * o.dtype.itemsize for o in outs)
    spaces = spaces or [SMEM] + [VMEM] * (len(operands) - 1)
    return pl.pallas_call(
        kernel,
        out_shape=tuple(outs),
        in_specs=[pl.BlockSpec(memory_space=space) for space in spaces],
        out_specs=tuple(pl.BlockSpec(memory_space=VMEM) for _ in outs),
        scratch_shapes=scratch,
        compiler_params=pltpu.CompilerParams(vmem_limit_bytes=limit),
        cost_estimate=pl.CostEstimate(flops=flops, bytes_accessed=moved, transcendentals=0),
    )(*operands)


def on_device(
    length,
    prefix_cache,
    tail_cache,
    ancestors,
    queries,
    fresh_kv,
    prompt_ids,
    sampled_ids,
    twist_table,
    readout,
):
    steps, count, width = queries.shape
    rows = steps * width // HEAD
    assert rows <= LANES and steps % 2 == 0
    cores = lax.axis_size("tensor")
    both = ("particle", "tensor")
    plans = exchanges(length, cores)
    asked = []
    for _, _, pairs in plans:
        asked.append(lax.ppermute(queries, both, pairs))
    reply = jax.ShapeDtypeStruct((count * rows + 4 * count, HEAD), jnp.int16)
    tail_work = 4 * steps * count * width * tail_cache.shape[2]
    local_work = 4 * steps * count * width * prefix_cache.shape[1]
    own, tails, ancestors = call(
        functools.partial(serve_own_kernel, length),
        [
            reply,
            jax.ShapeDtypeStruct(tail_cache.shape, tail_cache.dtype),
            jax.ShapeDtypeStruct(ancestors.shape, ancestors.dtype),
        ],
        [ancestors, queries, tail_cache, ancestors],
        tail_work,
        scratch=(pltpu.SemaphoreType.DMA((2,)),),
    )
    answer = own
    answers = [own]
    for (reach, parity, pairs), question in zip(plans, asked):
        (answer,) = call(
            functools.partial(serve_kernel, length, reach, parity),
            [reply],
            [ancestors, question, tails, answer],
            tail_work,
            spaces=[SMEM, VMEM, VMEM, pl.ANY],
        )
        answers.append(lax.ppermute(answer, both, pairs))
    local, logs = call(
        local_kernel,
        [jax.ShapeDtypeStruct(queries.shape, F32), jax.ShapeDtypeStruct((count, LANES), F32)],
        [queries, prefix_cache, fresh_kv],
        local_work,
        spaces=[VMEM] * 3,
    )
    repeats = jnp.sum(
        (sampled_ids[:, :, None] == prompt_ids[None, None, :]).astype(jnp.int32), axis=-1
    )
    looked_up = twist_table.at[sampled_ids].get(
        mode="promise_in_bounds", wrap_negative_indices=False
    )
    base = (looked_up - 2.0 * repeats.astype(F32)) * (1.0 / cores)
    attended, partial_value = call(
        functools.partial(combine_kernel, length, [plan[:2] for plan in plans]),
        [jax.ShapeDtypeStruct(queries.shape, BF16), jax.ShapeDtypeStruct((steps, count), F32)],
        [ancestors, local, logs, readout.reshape(1, width), base] + answers,
        16 * steps * count * width,
    )
    if cores == 2:
        twists = partial_value + lax.ppermute(partial_value, "tensor", [(0, 1), (1, 0)])
    else:
        twists = lax.psum(partial_value, "tensor")
    return (attended, twists)


def layer(length, *arguments):
    return on_device(length, *arguments)


def solution(mesh):
    return jax.shard_map(
        functools.partial(layer, mesh.shape["particle"]),
        mesh=mesh,
        in_specs=(
            P(None, "groups", "tensor"),
            P(None, ("groups", "particle"), None, "tensor"),
            P("groups"),
            P(None, ("groups", "particle"), "tensor"),
            P(None, None, ("groups", "particle"), "tensor"),
            P("groups"),
            P(None, ("groups", "particle")),
            P(),
            P("tensor"),
        ),
        out_specs=(P(None, ("groups", "particle"), "tensor"), P(None, ("groups", "particle"))),
        check_vma=False,
    )
```

```python
import functools
import math

import jax
import jax.numpy as jnp
from jax import lax
from jax.experimental import pallas as pl
from jax.experimental.pallas import tpu as pltpu
from jax.sharding import PartitionSpec as P


HEADS = 64
KV_HEADS = 8
HEAD = 128
EXCHANGES = ((1, 0), (2, 0), (2, 1), (1, 1))
GROUP = HEADS // KV_HEADS
EXPONENT_SCALE = math.log2(math.e) / math.sqrt(HEAD)

NEG_FILL = -1e30
LOG_STEPS = 32.0
LOG_FRACTION = 65534.0
TOP_CODE = 32000.0
TINY = 1e-30
LANES = 128

F32 = jnp.float32
BF16 = jnp.bfloat16
VMEM = pltpu.MemorySpace.VMEM
SMEM = pltpu.MemorySpace.SMEM


def exchanges(length, cores):
    found = []
    for reach, parity in EXCHANGES:
        partner = list(range(length))
        for i in range(length - reach):
            if (i // reach) % 2 == parity:
                partner[i], partner[i + reach] = i + reach, i
        pairs = []
        for i, other in enumerate(partner):
            turn = 1 if other == i else 0
            pairs += [(i * cores + c, other * cores + (c + turn) % cores) for c in range(cores)]
        found.append((reach, parity, pairs))
    return found


def partner_of(index, reach, parity):
    return jnp.where((index // reach) % 2 == parity, index + reach, index - reach)


def held_by(ancestors_ref, owner, holder, length, count):
    safe = jnp.clip(owner, 0, length - 1)
    exists = safe == owner
    found = []
    for p in range(count):
        slot = ancestors_ref[safe * count + p] - holder * count
        found.append((exists & (slot >= 0) & (slot < count), jnp.clip(slot, 0, count - 1)))
    return found


def head_tiles(query_ref, base):
    return [
        query_ref[t, :, base + g * HEAD : base + (g + 1) * HEAD].astype(F32)
        for t in range(query_ref.shape[0])
        for g in range(GROUP)
    ]


def scores_of(rows, keys):
    return lax.dot_general(rows, keys, (((1,), (1,)), ((), ())), preferred_element_type=F32)


def softmax_terms(scores):
    top = jnp.max(scores, axis=-1, keepdims=True)
    expo = jnp.exp2((scores - top) * EXPONENT_SCALE)
    return top, expo, jnp.sum(expo, axis=-1, keepdims=True)


def two_codes(value):
    value = value * LOG_STEPS
    whole = jnp.round(value)
    return whole, jnp.round((value - whole) * LOG_FRACTION)


def from_codes(whole, part):
    return (whole + part * (1.0 / LOG_FRACTION)) * (1.0 / LOG_STEPS)


def serve(slots, query_ref, key_ref, value_ref, out_ref):
    steps, count = query_ref.shape[0], query_ref.shape[1]
    heads = value_ref.shape[2] // HEAD
    many = steps * GROUP
    each = heads * many
    lane = lax.broadcasted_iota(jnp.int32, (GROUP, LANES), 1)
    row = lax.broadcasted_iota(jnp.int32, (GROUP, LANES), 0)
    notes = [[jnp.zeros((GROUP, LANES), F32) for _ in range(count)] for _ in range(3)]
    scores = []
    for k in range(heads):
        tiles = jnp.stack(head_tiles(query_ref, k * GROUP * HEAD), axis=0)
        rows = jnp.swapaxes(tiles, 0, 1).astype(BF16)
        cols = slice(k * HEAD, (k + 1) * HEAD)
        scores += [
            jnp.dot(rows[p], key_ref[slots[p], cols, :], preferred_element_type=F32)
            for p in range(count)
        ]
    terms = [softmax_terms(score) for score in scores]
    outs = [
        jnp.dot(
            terms[k * count + p][1].astype(BF16),
            value_ref[slots[p], :, k * HEAD : (k + 1) * HEAD],
            preferred_element_type=F32,
        )
        for k in range(heads)
        for p in range(count)
    ]
    for k in range(heads):
        for p in range(count):
            top, _, total = terms[k * count + p]
            out = outs[k * count + p]
            largest = jnp.maximum(jnp.max(jnp.abs(out), axis=-1, keepdims=True), TINY)
            code = jnp.round(out * (TOP_CODE / largest)).astype(jnp.int32)
            at = p * each + k * many
            out_ref[at : at + many, :] = code.astype(jnp.int16)
            for t in range(steps):
                here = lane == row + (k * many + t * GROUP)
                part = slice(t * GROUP, (t + 1) * GROUP)
                for note, column in zip(notes, (top, total, largest)):
                    note[p] = jnp.where(here, column[part], note[p])
    top, total, largest = (
        jnp.concatenate([jnp.sum(n, axis=0, keepdims=True) for n in note], axis=0) for note in notes
    )
    if each < LANES:
        total, largest = jnp.maximum(total, TINY), jnp.maximum(largest, TINY)
    spread = jnp.log2(total)
    level = two_codes(top * EXPONENT_SCALE + spread)
    scale = two_codes(jnp.log2(largest) - spread - math.log2(TOP_CODE))
    coded = jnp.concatenate(level + scale, axis=0).astype(jnp.int32)
    out_ref[count * each :, :] = coded.astype(jnp.int16)


def serve_kernel(length, reach, parity, ancestors_ref, query_ref, key_ref, value_ref, _, out_ref):
    count = query_ref.shape[1]
    me = lax.axis_index("particle")
    found = held_by(ancestors_ref, partner_of(me, reach, parity), me, length, count)
    serve([slot for _, slot in found], query_ref, key_ref, value_ref, out_ref)


def serve_own_kernel(
    length,
    ancestors_ref,
    query_ref,
    tail_ref,
    list_ref,
    out_ref,
    key_ref,
    value_ref,
    list_out,
    sems,
):
    copies = [
        pltpu.make_async_copy(tail_ref.at[1], value_ref, sems.at[0]),
        pltpu.make_async_copy(list_ref, list_out, sems.at[1]),
    ]
    for copy in copies:
        copy.start()
    count = query_ref.shape[1]
    me = lax.axis_index("particle")
    found = held_by(ancestors_ref, me, me, length, count)
    for j in range(count):
        for at in range(0, tail_ref.shape[3], HEAD):
            key_ref[j, at : at + HEAD, :] = tail_ref[0, j, :, at : at + HEAD].T
    serve([slot for _, slot in found], query_ref, key_ref, tail_ref.at[1], out_ref)
    for copy in copies:
        copy.wait()


def local_kernel(query_ref, prefix_ref, fresh_ref, out_ref, log_ref):
    steps, count = query_ref.shape[0], query_ref.shape[1]
    heads = prefix_ref.shape[2] // HEAD
    many = steps * GROUP
    lane = lax.broadcasted_iota(jnp.int32, (count, LANES), 1)
    logs = []
    for k in range(heads):
        cols = slice(k * HEAD, (k + 1) * HEAD)
        rows = jnp.concatenate(head_tiles(query_ref, k * GROUP * HEAD), axis=0).astype(BF16)
        top1, expo1, total1 = softmax_terms(scores_of(rows, prefix_ref[0, :, cols]))
        out1 = jnp.dot(expo1.astype(BF16), prefix_ref[1, :, cols], preferred_element_type=F32)
        fresh_keys = jnp.concatenate([fresh_ref[0, s, :, cols].astype(F32) for s in range(steps)], axis=0)
        fresh_values = jnp.concatenate([fresh_ref[1, s, :, cols].astype(F32) for s in range(steps)], axis=0)
        scores2 = scores_of(rows, fresh_keys.astype(BF16))
        row = lax.broadcasted_iota(jnp.int32, scores2.shape, 0)
        col = lax.broadcasted_iota(jnp.int32, scores2.shape, 1)
        seen = (row % count == col % count) & (col // count <= row // (GROUP * count))
        top2, expo2, total2 = softmax_terms(jnp.where(seen, scores2, NEG_FILL))
        out2 = jnp.dot(expo2.astype(BF16), fresh_values.astype(BF16), preferred_element_type=F32)
        top = jnp.maximum(top1, top2)
        share1 = jnp.exp2((top1 - top) * EXPONENT_SCALE)
        share2 = jnp.exp2((top2 - top) * EXPONENT_SCALE)
        total = share1 * total1 + share2 * total2
        context = (share1 * out1 + share2 * out2) / total
        context = context.reshape(many, count, HEAD)
        top, total = top.reshape(many, count, 1), total.reshape(many, count, 1)
        held = [jnp.zeros((count, LANES), F32) for _ in range(2)]
        for t in range(steps):
            for g in range(GROUP):
                at = (k * GROUP + g) * HEAD
                r = t * GROUP + g
                out_ref[t, :, at : at + HEAD] = context[r]
                held[0] = jnp.where(lane == k * many + r, top[r], held[0])
                held[1] = jnp.where(lane == k * many + r, total[r], held[1])
        inside = (lane >= k * many) & (lane < (k + 1) * many)
        level = held[0] * EXPONENT_SCALE + jnp.log2(jnp.where(inside, held[1], 1.0))
        logs.append(level)
    log_ref[...] = functools.reduce(jnp.add, logs)


def combine_kernel(length, plans, ancestors_ref, local_ref, log_ref, readout_ref, base_ref, *refs):
    sent_refs, (out_ref, twist_ref) = refs[: len(plans) + 1], refs[len(plans) + 1 :]
    steps, count = local_ref.shape[0], local_ref.shape[1]
    heads = local_ref.shape[2] // (HEAD * GROUP)
    many = steps * GROUP
    each = heads * many
    me = lax.axis_index("particle")
    source = [jnp.int32(0)] * count
    for m, (reach, parity) in enumerate(plans):
        found = held_by(ancestors_ref, me, partner_of(me, reach, parity), length, count)
        source = [jnp.where(here, m + 1, old) for (here, _), old in zip(found, source)]
    row = lax.broadcasted_iota(jnp.int32, (count, LANES), 0)
    lane = lax.broadcasted_iota(jnp.int32, (count, LANES), 1)

    def notes_of(ref):
        notes = ref[count * each :, :].astype(jnp.int32).astype(F32)
        return [notes[i * count : (i + 1) * count] for i in range(4)]

    sources = jnp.zeros((count, LANES), jnp.int32)
    for p in range(count):
        sources = jnp.where(row == p, source[p], sources)
    notes = notes_of(sent_refs[0])
    for m, ref in enumerate(sent_refs[1:], 1):
        notes = [jnp.where(sources == m, new, old) for new, old in zip(notes_of(ref), notes)]
    remote_level, scale = from_codes(*notes[:2]), from_codes(*notes[2:])
    local_level = log_ref[...]
    level = jnp.maximum(local_level, remote_level)
    local_share = jnp.exp2(local_level - level)
    remote_share = jnp.exp2(remote_level - level)
    total = local_share + remote_share
    local_share = local_share / total
    remote_share = remote_share / total * jnp.exp2(scale)
    gathered = [jnp.zeros((count, HEAD), F32) for _ in range(steps)]
    for k in range(heads):
        for pair in range(steps // 2):
            at = k * many + pair * 2 * GROUP
            picked = []
            for p in range(count):
                here = slice(p * each + at, p * each + at + 2 * GROUP)
                code = sent_refs[0][here, :]
                for m, ref in enumerate(sent_refs[1:], 1):
                    code = jnp.where(source[p] == m, ref[here, :], code)
                picked.append(code.astype(jnp.int32).astype(F32))
            tiles = jnp.swapaxes(jnp.stack(picked, axis=0), 0, 1)
            for r in range(2 * GROUP):
                t, h = pair * 2 + r // GROUP, k * GROUP + r % GROUP
                cols = slice(h * HEAD, (h + 1) * HEAD)
                context = local_share[:, at + r : at + r + 1] * local_ref[t, :, cols]
                context = context + remote_share[:, at + r : at + r + 1] * tiles[r]
                out_ref[t, :, cols] = context.astype(BF16)
                gathered[t] = gathered[t] + context * readout_ref[:, cols]
    for t in range(steps):
        column = jnp.sum(gathered[t], axis=-1, keepdims=True)
        line = jnp.sum(jnp.where(row == lane, column, 0.0), axis=0, keepdims=True)
        twist_ref[t : t + 1, :] = line[:, :count] + base_ref[t : t + 1, :]


def call(kernel, outs, operands, flops, spaces=None, scratch=(), limit=24 << 20):
    moved = sum(math.prod(o.shape) * o.dtype.itemsize for o in operands)
    moved += sum(math.prod(o.shape) * o.dtype.itemsize for o in outs)
    spaces = spaces or [SMEM] + [VMEM] * (len(operands) - 1)
    return pl.pallas_call(
        kernel,
        out_shape=tuple(outs),
        in_specs=[pl.BlockSpec(memory_space=space) for space in spaces],
        out_specs=tuple(pl.BlockSpec(memory_space=VMEM) for _ in outs),
        scratch_shapes=scratch,
        compiler_params=pltpu.CompilerParams(vmem_limit_bytes=limit),
        cost_estimate=pl.CostEstimate(flops=flops, bytes_accessed=moved, transcendentals=0),
    )(*operands)


def on_device(
    length,
    prefix_cache,
    tail_cache,
    ancestors,
    queries,
    fresh_kv,
    prompt_ids,
    sampled_ids,
    twist_table,
    readout,
):
    steps, count, width = queries.shape
    rows = steps * width // HEAD
    tail_width = tail_cache.shape[3]
    assert rows <= LANES and steps % 2 == 0
    cores = lax.axis_size("tensor")
    both = ("particle", "tensor")
    plans = exchanges(length, cores)
    asked = []
    for _, _, pairs in plans:
        asked.append(lax.ppermute(queries, both, pairs))
    reply = jax.ShapeDtypeStruct((count * rows + 4 * count, HEAD), jnp.int16)
    tail_work = 4 * steps * count * width * tail_cache.shape[2]
    local_work = 4 * steps * count * width * prefix_cache.shape[1]
    own, keys, values, ancestors = call(
        functools.partial(serve_own_kernel, length),
        [
            reply,
            jax.ShapeDtypeStruct((count, tail_width, tail_cache.shape[2]), BF16),
            jax.ShapeDtypeStruct(tail_cache.shape[1:], BF16),
            jax.ShapeDtypeStruct(ancestors.shape, ancestors.dtype),
        ],
        [ancestors, queries, tail_cache, ancestors],
        tail_work,
        scratch=(pltpu.SemaphoreType.DMA((2,)),),
    )
    answer = own
    answers = [own]
    for (reach, parity, pairs), question in zip(plans, asked):
        (answer,) = call(
            functools.partial(serve_kernel, length, reach, parity),
            [reply],
            [ancestors, question, keys, values, answer],
            tail_work,
            spaces=[SMEM, VMEM, VMEM, VMEM, pl.ANY],
        )
        answers.append(lax.ppermute(answer, both, pairs))
    local, logs = call(
        local_kernel,
        [jax.ShapeDtypeStruct(queries.shape, F32), jax.ShapeDtypeStruct((count, LANES), F32)],
        [queries, prefix_cache, fresh_kv],
        local_work,
        spaces=[VMEM] * 3,
    )
    repeats = jnp.sum(
        (sampled_ids[:, :, None] == prompt_ids[None, None, :]).astype(jnp.int32), axis=-1
    )
    looked_up = twist_table.at[sampled_ids].get(
        mode="promise_in_bounds", wrap_negative_indices=False
    )
    base = (looked_up - 2.0 * repeats.astype(F32)) * (1.0 / cores)
    attended, partial_value = call(
        functools.partial(combine_kernel, length, [plan[:2] for plan in plans]),
        [jax.ShapeDtypeStruct(queries.shape, BF16), jax.ShapeDtypeStruct((steps, count), F32)],
        [ancestors, local, logs, readout.reshape(1, width), base] + answers,
        16 * steps * count * width,
    )
    if cores == 2:
        twists = partial_value + lax.ppermute(partial_value, "tensor", [(0, 1), (1, 0)])
    else:
        twists = lax.psum(partial_value, "tensor")
    return (attended, twists)


def layer(length, *arguments):
    return on_device(length, *arguments)


def solution(mesh):
    return jax.shard_map(
        functools.partial(layer, mesh.shape["particle"]),
        mesh=mesh,
        in_specs=(
            P(None, "groups", "tensor"),
            P(None, ("groups", "particle"), None, "tensor"),
            P("groups"),
            P(None, ("groups", "particle"), "tensor"),
            P(None, None, ("groups", "particle"), "tensor"),
            P("groups"),
            P(None, ("groups", "particle")),
            P(),
            P("tensor"),
        ),
        out_specs=(P(None, ("groups", "particle"), "tensor"), P(None, ("groups", "particle"))),
        check_vma=False,
    )
```

```python
import functools
import math

import jax
import jax.numpy as jnp
from jax import lax
from jax.experimental import pallas as pl
from jax.experimental.pallas import tpu as pltpu
from jax.sharding import PartitionSpec as P


HEADS = 64
KV_HEADS = 8
HEAD = 128
EXCHANGES = ((1, 0), (2, 0), (2, 1), (1, 1))
GROUP = HEADS // KV_HEADS
EXPONENT_SCALE = math.log2(math.e) / math.sqrt(HEAD)

NEG_FILL = -1e30
LOG_STEPS = 32.0
LOG_FRACTION = 65534.0
TOP_CODE = 32000.0
TINY = 1e-30
LANES = 128

F32 = jnp.float32
BF16 = jnp.bfloat16
VMEM = pltpu.MemorySpace.VMEM
SMEM = pltpu.MemorySpace.SMEM


def exchanges(length, cores):
    found = []
    for reach, parity in EXCHANGES:
        partner = list(range(length))
        for i in range(length - reach):
            if (i // reach) % 2 == parity:
                partner[i], partner[i + reach] = i + reach, i
        pairs = []
        for i, other in enumerate(partner):
            turn = 1 if other == i else 0
            pairs += [(i * cores + c, other * cores + (c + turn) % cores) for c in range(cores)]
        found.append((reach, parity, pairs))
    return found


def partner_of(index, reach, parity):
    return jnp.where((index // reach) % 2 == parity, index + reach, index - reach)


def held_by(ancestors_ref, owner, holder, length, count):
    safe = jnp.clip(owner, 0, length - 1)
    exists = safe == owner
    found = []
    for p in range(count):
        slot = ancestors_ref[safe * count + p] - holder * count
        found.append((exists & (slot >= 0) & (slot < count), jnp.clip(slot, 0, count - 1)))
    return found


def head_tiles(query_ref, base):
    return [
        query_ref[t, :, base + g * HEAD : base + (g + 1) * HEAD].astype(F32)
        for t in range(query_ref.shape[0])
        for g in range(GROUP)
    ]


def scores_of(rows, keys):
    return lax.dot_general(rows, keys, (((1,), (1,)), ((), ())), preferred_element_type=F32)


def softmax_terms(scores):
    top = jnp.max(scores, axis=-1, keepdims=True)
    expo = jnp.exp2((scores - top) * EXPONENT_SCALE)
    return top, expo, jnp.sum(expo, axis=-1, keepdims=True)


def two_codes(value):
    value = value * LOG_STEPS
    whole = jnp.round(value)
    return whole, jnp.round((value - whole) * LOG_FRACTION)


def from_codes(whole, part):
    return (whole + part * (1.0 / LOG_FRACTION)) * (1.0 / LOG_STEPS)


def serve(slots, query_ref, key_ref, value_ref, out_ref):
    steps, count = query_ref.shape[0], query_ref.shape[1]
    heads = value_ref.shape[2] // HEAD
    many = steps * GROUP
    each = heads * many
    lane = lax.broadcasted_iota(jnp.int32, (GROUP, LANES), 1)
    row = lax.broadcasted_iota(jnp.int32, (GROUP, LANES), 0)
    notes = [[jnp.zeros((GROUP, LANES), F32) for _ in range(count)] for _ in range(3)]
    scores = []
    for k in range(heads):
        tiles = jnp.stack(head_tiles(query_ref, k * GROUP * HEAD), axis=0)
        rows = jnp.swapaxes(tiles, 0, 1).astype(BF16)
        cols = slice(k * HEAD, (k + 1) * HEAD)
        scores += [
            jnp.dot(rows[p], key_ref[slots[p], cols, :], preferred_element_type=F32)
            for p in range(count)
        ]
    terms = [softmax_terms(score) for score in scores]
    outs = [
        jnp.dot(
            terms[k * count + p][1].astype(BF16),
            value_ref[slots[p], :, k * HEAD : (k + 1) * HEAD],
            preferred_element_type=F32,
        )
        for k in range(heads)
        for p in range(count)
    ]
    for k in range(heads):
        for p in range(count):
            top, _, total = terms[k * count + p]
            out = outs[k * count + p]
            largest = jnp.maximum(jnp.max(jnp.abs(out), axis=-1, keepdims=True), TINY)
            code = jnp.round(out * (TOP_CODE / largest)).astype(jnp.int32)
            at = p * each + k * many
            out_ref[at : at + many, :] = code.astype(jnp.int16)
            for t in range(steps):
                here = lane == row + (k * many + t * GROUP)
                part = slice(t * GROUP, (t + 1) * GROUP)
                for note, column in zip(notes, (top, total, largest)):
                    note[p] = jnp.where(here, column[part], note[p])
    top, total, largest = (
        jnp.concatenate([jnp.sum(n, axis=0, keepdims=True) for n in note], axis=0) for note in notes
    )
    if each < LANES:
        total, largest = jnp.maximum(total, TINY), jnp.maximum(largest, TINY)
    spread = jnp.log2(total)
    level = two_codes(top * EXPONENT_SCALE + spread)
    scale = two_codes(jnp.log2(largest) - spread - math.log2(TOP_CODE))
    coded = jnp.concatenate(level + scale, axis=0).astype(jnp.int32)
    out_ref[count * each :, :] = coded.astype(jnp.int16)


def serve_kernel(length, reach, parity, ancestors_ref, query_ref, key_ref, value_ref, _, out_ref):
    count = query_ref.shape[1]
    me = lax.axis_index("particle")
    asker = partner_of(me, reach, parity) if reach else me
    found = held_by(ancestors_ref, asker, me, length, count)
    serve([slot for _, slot in found], query_ref, key_ref, value_ref, out_ref)


def prepare_kernel(tail_ref, list_ref, key_ref, value_ref, list_out, sems):
    copies = [
        pltpu.make_async_copy(tail_ref.at[1], value_ref, sems.at[0]),
        pltpu.make_async_copy(list_ref, list_out, sems.at[1]),
    ]
    for copy in copies:
        copy.start()
    for j in range(tail_ref.shape[1]):
        for at in range(0, tail_ref.shape[3], HEAD):
            key_ref[j, at : at + HEAD, :] = tail_ref[0, j, :, at : at + HEAD].T
    for copy in copies:
        copy.wait()


def local_kernel(query_ref, prefix_ref, fresh_ref, out_ref, log_ref):
    steps, count = query_ref.shape[0], query_ref.shape[1]
    heads = prefix_ref.shape[2] // HEAD
    many = steps * GROUP
    lane = lax.broadcasted_iota(jnp.int32, (count, LANES), 1)
    logs = []
    for k in range(heads):
        cols = slice(k * HEAD, (k + 1) * HEAD)
        rows = jnp.concatenate(head_tiles(query_ref, k * GROUP * HEAD), axis=0).astype(BF16)
        top1, expo1, total1 = softmax_terms(scores_of(rows, prefix_ref[0, :, cols]))
        out1 = jnp.dot(expo1.astype(BF16), prefix_ref[1, :, cols], preferred_element_type=F32)
        fresh_keys = jnp.concatenate([fresh_ref[0, s, :, cols].astype(F32) for s in range(steps)], axis=0)
        fresh_values = jnp.concatenate([fresh_ref[1, s, :, cols].astype(F32) for s in range(steps)], axis=0)
        scores2 = scores_of(rows, fresh_keys.astype(BF16))
        row = lax.broadcasted_iota(jnp.int32, scores2.shape, 0)
        col = lax.broadcasted_iota(jnp.int32, scores2.shape, 1)
        seen = (row % count == col % count) & (col // count <= row // (GROUP * count))
        top2, expo2, total2 = softmax_terms(jnp.where(seen, scores2, NEG_FILL))
        out2 = jnp.dot(expo2.astype(BF16), fresh_values.astype(BF16), preferred_element_type=F32)
        top = jnp.maximum(top1, top2)
        share1 = jnp.exp2((top1 - top) * EXPONENT_SCALE)
        share2 = jnp.exp2((top2 - top) * EXPONENT_SCALE)
        total = share1 * total1 + share2 * total2
        context = (share1 * out1 + share2 * out2) / total
        context = context.reshape(many, count, HEAD)
        top, total = top.reshape(many, count, 1), total.reshape(many, count, 1)
        held = [jnp.zeros((count, LANES), F32) for _ in range(2)]
        for t in range(steps):
            for g in range(GROUP):
                at = (k * GROUP + g) * HEAD
                r = t * GROUP + g
                out_ref[t, :, at : at + HEAD] = context[r]
                held[0] = jnp.where(lane == k * many + r, top[r], held[0])
                held[1] = jnp.where(lane == k * many + r, total[r], held[1])
        inside = (lane >= k * many) & (lane < (k + 1) * many)
        level = held[0] * EXPONENT_SCALE + jnp.log2(jnp.where(inside, held[1], 1.0))
        logs.append(level)
    log_ref[...] = functools.reduce(jnp.add, logs)


def combine_kernel(length, plans, ancestors_ref, local_ref, log_ref, readout_ref, base_ref, *refs):
    sent_refs, (out_ref, twist_ref) = refs[: len(plans) + 1], refs[len(plans) + 1 :]
    steps, count = local_ref.shape[0], local_ref.shape[1]
    heads = local_ref.shape[2] // (HEAD * GROUP)
    many = steps * GROUP
    each = heads * many
    me = lax.axis_index("particle")
    source = [jnp.int32(0)] * count
    for m, (reach, parity) in enumerate(plans):
        found = held_by(ancestors_ref, me, partner_of(me, reach, parity), length, count)
        source = [jnp.where(here, m + 1, old) for (here, _), old in zip(found, source)]
    row = lax.broadcasted_iota(jnp.int32, (count, LANES), 0)
    lane = lax.broadcasted_iota(jnp.int32, (count, LANES), 1)

    def notes_of(ref):
        notes = ref[count * each :, :].astype(jnp.int32).astype(F32)
        return [notes[i * count : (i + 1) * count] for i in range(4)]

    sources = jnp.zeros((count, LANES), jnp.int32)
    for p in range(count):
        sources = jnp.where(row == p, source[p], sources)
    notes = notes_of(sent_refs[0])
    for m, ref in enumerate(sent_refs[1:], 1):
        notes = [jnp.where(sources == m, new, old) for new, old in zip(notes_of(ref), notes)]
    remote_level, scale = from_codes(*notes[:2]), from_codes(*notes[2:])
    local_level = log_ref[...]
    level = jnp.maximum(local_level, remote_level)
    local_share = jnp.exp2(local_level - level)
    remote_share = jnp.exp2(remote_level - level)
    total = local_share + remote_share
    local_share = local_share / total
    remote_share = remote_share / total * jnp.exp2(scale)
    gathered = [jnp.zeros((count, HEAD), F32) for _ in range(steps)]
    for k in range(heads):
        for pair in range(steps // 2):
            at = k * many + pair * 2 * GROUP
            picked = []
            for p in range(count):
                here = slice(p * each + at, p * each + at + 2 * GROUP)
                code = sent_refs[0][here, :]
                for m, ref in enumerate(sent_refs[1:], 1):
                    code = jnp.where(source[p] == m, ref[here, :], code)
                picked.append(code.astype(jnp.int32).astype(F32))
            tiles = jnp.swapaxes(jnp.stack(picked, axis=0), 0, 1)
            for r in range(2 * GROUP):
                t, h = pair * 2 + r // GROUP, k * GROUP + r % GROUP
                cols = slice(h * HEAD, (h + 1) * HEAD)
                context = local_share[:, at + r : at + r + 1] * local_ref[t, :, cols]
                context = context + remote_share[:, at + r : at + r + 1] * tiles[r]
                out_ref[t, :, cols] = context.astype(BF16)
                gathered[t] = gathered[t] + context * readout_ref[:, cols]
    for t in range(steps):
        column = jnp.sum(gathered[t], axis=-1, keepdims=True)
        line = jnp.sum(jnp.where(row == lane, column, 0.0), axis=0, keepdims=True)
        twist_ref[t : t + 1, :] = line[:, :count] + base_ref[t : t + 1, :]


def call(kernel, outs, operands, flops, spaces=None, scratch=(), limit=24 << 20):
    moved = sum(math.prod(o.shape) * o.dtype.itemsize for o in operands)
    moved += sum(math.prod(o.shape) * o.dtype.itemsize for o in outs)
    spaces = spaces or [SMEM] + [VMEM] * (len(operands) - 1)
    return pl.pallas_call(
        kernel,
        out_shape=tuple(outs),
        in_specs=[pl.BlockSpec(memory_space=space) for space in spaces],
        out_specs=tuple(pl.BlockSpec(memory_space=VMEM) for _ in outs),
        scratch_shapes=scratch,
        compiler_params=pltpu.CompilerParams(vmem_limit_bytes=limit),
        cost_estimate=pl.CostEstimate(flops=flops, bytes_accessed=moved, transcendentals=0),
    )(*operands)


def on_device(
    length,
    prefix_cache,
    tail_cache,
    ancestors,
    queries,
    fresh_kv,
    prompt_ids,
    sampled_ids,
    twist_table,
    readout,
):
    steps, count, width = queries.shape
    rows = steps * width // HEAD
    tail_width = tail_cache.shape[3]
    assert rows <= LANES and steps % 2 == 0
    cores = lax.axis_size("tensor")
    both = ("particle", "tensor")
    plans = exchanges(length, cores)
    asked = []
    for _, _, pairs in plans:
        asked.append(lax.ppermute(queries, both, pairs))
    reply = jax.ShapeDtypeStruct((count * rows + 4 * count, HEAD), jnp.int16)
    tail_work = 4 * steps * count * width * tail_cache.shape[2]
    local_work = 4 * steps * count * width * prefix_cache.shape[1]
    keys, values, ancestors = call(
        prepare_kernel,
        [
            jax.ShapeDtypeStruct((count, tail_width, tail_cache.shape[2]), BF16),
            jax.ShapeDtypeStruct(tail_cache.shape[1:], BF16),
            jax.ShapeDtypeStruct(ancestors.shape, ancestors.dtype),
        ],
        [tail_cache, ancestors],
        0,
        spaces=[VMEM] * 2,
        scratch=(pltpu.SemaphoreType.DMA((2,)),),
    )
    answer = ancestors
    answers = []

    def reply_to(reach, parity, question, before):
        (answer,) = call(
            functools.partial(serve_kernel, length, reach, parity),
            [reply],
            [ancestors, question, keys, values, before],
            tail_work,
            spaces=[SMEM, VMEM, VMEM, VMEM, pl.ANY],
        )
        return answer

    for (reach, parity, pairs), question in zip(plans, asked):
        answer = reply_to(reach, parity, question, answer)
        answers.append(lax.ppermute(answer, both, pairs))
    answers.insert(0, reply_to(0, 0, queries, answer))
    local, logs = call(
        local_kernel,
        [jax.ShapeDtypeStruct(queries.shape, F32), jax.ShapeDtypeStruct((count, LANES), F32)],
        [queries, prefix_cache, fresh_kv],
        local_work,
        spaces=[VMEM] * 3,
    )
    repeats = jnp.sum(
        (sampled_ids[:, :, None] == prompt_ids[None, None, :]).astype(jnp.int32), axis=-1
    )
    looked_up = twist_table.at[sampled_ids].get(
        mode="promise_in_bounds", wrap_negative_indices=False
    )
    base = (looked_up - 2.0 * repeats.astype(F32)) * (1.0 / cores)
    attended, partial_value = call(
        functools.partial(combine_kernel, length, [plan[:2] for plan in plans]),
        [jax.ShapeDtypeStruct(queries.shape, BF16), jax.ShapeDtypeStruct((steps, count), F32)],
        [ancestors, local, logs, readout.reshape(1, width), base] + answers,
        16 * steps * count * width,
    )
    if cores == 2:
        twists = partial_value + lax.ppermute(partial_value, "tensor", [(0, 1), (1, 0)])
    else:
        twists = lax.psum(partial_value, "tensor")
    return (attended, twists)


def layer(length, *arguments):
    return on_device(length, *arguments)


def solution(mesh):
    return jax.shard_map(
        functools.partial(layer, mesh.shape["particle"]),
        mesh=mesh,
        in_specs=(
            P(None, "groups", "tensor"),
            P(None, ("groups", "particle"), None, "tensor"),
            P("groups"),
            P(None, ("groups", "particle"), "tensor"),
            P(None, None, ("groups", "particle"), "tensor"),
            P("groups"),
            P(None, ("groups", "particle")),
            P(),
            P("tensor"),
        ),
        out_specs=(P(None, ("groups", "particle"), "tensor"), P(None, ("groups", "particle"))),
        check_vma=False,
    )
```

```python
import functools
import math

import jax
import jax.numpy as jnp
from jax import lax
from jax.experimental import pallas as pl
from jax.experimental.pallas import tpu as pltpu
from jax.sharding import PartitionSpec as P


HEADS = 64
KV_HEADS = 8
HEAD = 128
EXCHANGES = ((1, 0), (2, 0), (2, 1), (1, 1))
GROUP = HEADS // KV_HEADS
EXPONENT_SCALE = math.log2(math.e) / math.sqrt(HEAD)

NEG_FILL = -1e30
LOG_STEPS = 32.0
LOG_FRACTION = 65534.0
TOP_CODE = 32000.0
TINY = 1e-30
LANES = 128

F32 = jnp.float32
BF16 = jnp.bfloat16
VMEM = pltpu.MemorySpace.VMEM
SMEM = pltpu.MemorySpace.SMEM


def exchanges(length, cores):
    found = []
    for reach, parity in EXCHANGES:
        partner = list(range(length))
        for i in range(length - reach):
            if (i // reach) % 2 == parity:
                partner[i], partner[i + reach] = i + reach, i
        pairs = []
        for i, other in enumerate(partner):
            turn = 1 if other == i else 0
            pairs += [(i * cores + c, other * cores + (c + turn) % cores) for c in range(cores)]
        found.append((reach, parity, pairs))
    return found


def partner_of(index, reach, parity):
    return jnp.where((index // reach) % 2 == parity, index + reach, index - reach)


def held_by(ancestors_ref, owner, holder, length, count):
    safe = jnp.clip(owner, 0, length - 1)
    exists = safe == owner
    found = []
    for p in range(count):
        slot = ancestors_ref[safe * count + p] - holder * count
        found.append((exists & (slot >= 0) & (slot < count), jnp.clip(slot, 0, count - 1)))
    return found


def head_tiles(query_ref, base):
    return [
        query_ref[t, :, base + g * HEAD : base + (g + 1) * HEAD].astype(F32)
        for t in range(query_ref.shape[0])
        for g in range(GROUP)
    ]


def scores_of(rows, keys):
    return lax.dot_general(rows, keys, (((1,), (1,)), ((), ())), preferred_element_type=F32)


def softmax_terms(scores):
    top = jnp.max(scores, axis=-1, keepdims=True)
    expo = jnp.exp2((scores - top) * EXPONENT_SCALE)
    return top, expo, jnp.sum(expo, axis=-1, keepdims=True)


def two_codes(value):
    value = value * LOG_STEPS
    whole = jnp.round(value)
    return whole, jnp.round((value - whole) * LOG_FRACTION)


def from_codes(whole, part):
    return (whole + part * (1.0 / LOG_FRACTION)) * (1.0 / LOG_STEPS)


def serve(slots, query_ref, key_ref, value_ref, out_ref):
    steps, count = query_ref.shape[0], query_ref.shape[1]
    heads = value_ref.shape[2] // HEAD
    many = steps * GROUP
    each = heads * many
    lane = lax.broadcasted_iota(jnp.int32, (GROUP, LANES), 1)
    row = lax.broadcasted_iota(jnp.int32, (GROUP, LANES), 0)
    notes = [[jnp.zeros((GROUP, LANES), F32) for _ in range(count)] for _ in range(3)]
    scores = []
    for k in range(heads):
        tiles = jnp.stack(head_tiles(query_ref, k * GROUP * HEAD), axis=0)
        rows = jnp.swapaxes(tiles, 0, 1).astype(BF16)
        cols = slice(k * HEAD, (k + 1) * HEAD)
        scores += [
            jnp.dot(rows[p], key_ref[slots[p], cols, :], preferred_element_type=F32)
            for p in range(count)
        ]
    terms = [softmax_terms(score) for score in scores]

    def note(which, p, k, column):
        for t in range(steps):
            here = lane == row + (k * many + t * GROUP)
            part = column[t * GROUP : (t + 1) * GROUP]
            notes[which][p] = jnp.where(here, part, notes[which][p])

    def gather_notes(which):
        return jnp.concatenate([jnp.sum(n, axis=0, keepdims=True) for n in notes[which]], axis=0)

    for k in range(heads):
        for p in range(count):
            top, _, total = terms[k * count + p]
            note(0, p, k, top)
            note(1, p, k, total)
    top, total = gather_notes(0), gather_notes(1)
    if each < LANES:
        total = jnp.maximum(total, TINY)
    spread = jnp.log2(total)
    level = two_codes(top * EXPONENT_SCALE + spread)
    outs = [
        jnp.dot(
            terms[k * count + p][1].astype(BF16),
            value_ref[slots[p], :, k * HEAD : (k + 1) * HEAD],
            preferred_element_type=F32,
        )
        for k in range(heads)
        for p in range(count)
    ]
    for k in range(heads):
        for p in range(count):
            out = outs[k * count + p]
            largest = jnp.maximum(jnp.max(jnp.abs(out), axis=-1, keepdims=True), TINY)
            code = jnp.round(out * (TOP_CODE / largest)).astype(jnp.int32)
            at = p * each + k * many
            out_ref[at : at + many, :] = code.astype(jnp.int16)
            note(2, p, k, largest)
    largest = gather_notes(2)
    if each < LANES:
        largest = jnp.maximum(largest, TINY)
    scale = two_codes(jnp.log2(largest) - spread - math.log2(TOP_CODE))
    coded = jnp.concatenate(level + scale, axis=0).astype(jnp.int32)
    out_ref[count * each :, :] = coded.astype(jnp.int16)


def serve_kernel(length, reach, parity, ancestors_ref, query_ref, key_ref, value_ref, _, out_ref):
    count = query_ref.shape[1]
    me = lax.axis_index("particle")
    asker = partner_of(me, reach, parity) if reach else me
    found = held_by(ancestors_ref, asker, me, length, count)
    serve([slot for _, slot in found], query_ref, key_ref, value_ref, out_ref)


def prepare_kernel(tail_ref, list_ref, key_ref, value_ref, list_out, sems):
    copies = [
        pltpu.make_async_copy(tail_ref.at[1], value_ref, sems.at[0]),
        pltpu.make_async_copy(list_ref, list_out, sems.at[1]),
    ]
    for copy in copies:
        copy.start()
    for j in range(tail_ref.shape[1]):
        for at in range(0, tail_ref.shape[3], HEAD):
            key_ref[j, at : at + HEAD, :] = tail_ref[0, j, :, at : at + HEAD].T
    for copy in copies:
        copy.wait()


def local_kernel(query_ref, prefix_ref, fresh_ref, out_ref, log_ref):
    steps, count = query_ref.shape[0], query_ref.shape[1]
    heads = prefix_ref.shape[2] // HEAD
    many = steps * GROUP
    lane = lax.broadcasted_iota(jnp.int32, (count, LANES), 1)
    logs = []
    for k in range(heads):
        cols = slice(k * HEAD, (k + 1) * HEAD)
        rows = jnp.concatenate(head_tiles(query_ref, k * GROUP * HEAD), axis=0).astype(BF16)
        top1, expo1, total1 = softmax_terms(scores_of(rows, prefix_ref[0, :, cols]))
        out1 = jnp.dot(expo1.astype(BF16), prefix_ref[1, :, cols], preferred_element_type=F32)
        fresh_keys = jnp.concatenate([fresh_ref[0, s, :, cols].astype(F32) for s in range(steps)], axis=0)
        fresh_values = jnp.concatenate([fresh_ref[1, s, :, cols].astype(F32) for s in range(steps)], axis=0)
        scores2 = scores_of(rows, fresh_keys.astype(BF16))
        row = lax.broadcasted_iota(jnp.int32, scores2.shape, 0)
        col = lax.broadcasted_iota(jnp.int32, scores2.shape, 1)
        seen = (row % count == col % count) & (col // count <= row // (GROUP * count))
        top2, expo2, total2 = softmax_terms(jnp.where(seen, scores2, NEG_FILL))
        out2 = jnp.dot(expo2.astype(BF16), fresh_values.astype(BF16), preferred_element_type=F32)
        top = jnp.maximum(top1, top2)
        share1 = jnp.exp2((top1 - top) * EXPONENT_SCALE)
        share2 = jnp.exp2((top2 - top) * EXPONENT_SCALE)
        total = share1 * total1 + share2 * total2
        context = (share1 * out1 + share2 * out2) / total
        context = context.reshape(many, count, HEAD)
        top, total = top.reshape(many, count, 1), total.reshape(many, count, 1)
        held = [jnp.zeros((count, LANES), F32) for _ in range(2)]
        for t in range(steps):
            for g in range(GROUP):
                at = (k * GROUP + g) * HEAD
                r = t * GROUP + g
                out_ref[t, :, at : at + HEAD] = context[r]
                held[0] = jnp.where(lane == k * many + r, top[r], held[0])
                held[1] = jnp.where(lane == k * many + r, total[r], held[1])
        inside = (lane >= k * many) & (lane < (k + 1) * many)
        level = held[0] * EXPONENT_SCALE + jnp.log2(jnp.where(inside, held[1], 1.0))
        logs.append(level)
    log_ref[...] = functools.reduce(jnp.add, logs)


def combine_kernel(plans, ancestors_ref, local_ref, log_ref, readout_ref, base_ref, *refs):
    sent_refs, (out_ref, twist_ref) = refs[: len(plans) + 1], refs[len(plans) + 1 :]
    steps, count = local_ref.shape[0], local_ref.shape[1]
    heads = local_ref.shape[2] // (HEAD * GROUP)
    many = steps * GROUP
    each = heads * many
    me = lax.axis_index("particle")
    source = []
    for p in range(count):
        parent = lax.div(ancestors_ref[me * count + p], count)
        found = jnp.int32(0)
        for m, (reach, parity) in enumerate(plans):
            found = jnp.where(parent == partner_of(me, reach, parity), m + 1, found)
        source.append(found)
    row = lax.broadcasted_iota(jnp.int32, (count, LANES), 0)
    lane = lax.broadcasted_iota(jnp.int32, (count, LANES), 1)

    def notes_of(ref):
        notes = ref[count * each :, :].astype(jnp.int32).astype(F32)
        return [notes[i * count : (i + 1) * count] for i in range(4)]

    sources = jnp.zeros((count, LANES), jnp.int32)
    for p in range(count):
        sources = jnp.where(row == p, source[p], sources)
    notes = notes_of(sent_refs[0])
    for m, ref in enumerate(sent_refs[1:], 1):
        notes = [jnp.where(sources == m, new, old) for new, old in zip(notes_of(ref), notes)]
    remote_level, scale = from_codes(*notes[:2]), from_codes(*notes[2:])
    local_level = log_ref[...]
    level = jnp.maximum(local_level, remote_level)
    local_share = jnp.exp2(local_level - level)
    remote_share = jnp.exp2(remote_level - level)
    total = local_share + remote_share
    local_share = local_share / total
    remote_share = remote_share / total * jnp.exp2(scale)
    gathered = [jnp.zeros((count, HEAD), F32) for _ in range(steps)]
    for k in range(heads):
        for pair in range(steps // 2):
            at = k * many + pair * 2 * GROUP
            picked = []
            for p in range(count):
                here = slice(p * each + at, p * each + at + 2 * GROUP)
                code = sent_refs[0][here, :]
                for m, ref in enumerate(sent_refs[1:], 1):
                    code = jnp.where(source[p] == m, ref[here, :], code)
                picked.append(code.astype(jnp.int32).astype(F32))
            tiles = jnp.swapaxes(jnp.stack(picked, axis=0), 0, 1)
            for r in range(2 * GROUP):
                t, h = pair * 2 + r // GROUP, k * GROUP + r % GROUP
                cols = slice(h * HEAD, (h + 1) * HEAD)
                context = local_share[:, at + r : at + r + 1] * local_ref[t, :, cols]
                context = context + remote_share[:, at + r : at + r + 1] * tiles[r]
                out_ref[t, :, cols] = context.astype(BF16)
                gathered[t] = gathered[t] + context * readout_ref[:, cols]
    for t in range(steps):
        column = jnp.sum(gathered[t], axis=-1, keepdims=True)
        line = jnp.sum(jnp.where(row == lane, column, 0.0), axis=0, keepdims=True)
        twist_ref[t : t + 1, :] = line[:, :count] + base_ref[t : t + 1, :]


def call(kernel, outs, operands, flops, spaces=None, scratch=(), limit=24 << 20):
    moved = sum(math.prod(o.shape) * o.dtype.itemsize for o in operands)
    moved += sum(math.prod(o.shape) * o.dtype.itemsize for o in outs)
    spaces = spaces or [SMEM] + [VMEM] * (len(operands) - 1)
    return pl.pallas_call(
        kernel,
        out_shape=tuple(outs),
        in_specs=[pl.BlockSpec(memory_space=space) for space in spaces],
        out_specs=tuple(pl.BlockSpec(memory_space=VMEM) for _ in outs),
        scratch_shapes=scratch,
        compiler_params=pltpu.CompilerParams(vmem_limit_bytes=limit),
        cost_estimate=pl.CostEstimate(flops=flops, bytes_accessed=moved, transcendentals=0),
    )(*operands)


def on_device(
    length,
    prefix_cache,
    tail_cache,
    ancestors,
    queries,
    fresh_kv,
    prompt_ids,
    sampled_ids,
    twist_table,
    readout,
):
    steps, count, width = queries.shape
    rows = steps * width // HEAD
    tail_width = tail_cache.shape[3]
    assert rows <= LANES and steps % 2 == 0
    cores = lax.axis_size("tensor")
    both = ("particle", "tensor")
    plans = exchanges(length, cores)
    asked = []
    for _, _, pairs in plans:
        asked.append(lax.ppermute(queries, both, pairs))
    reply = jax.ShapeDtypeStruct((count * rows + 4 * count, HEAD), jnp.int16)
    tail_work = 4 * steps * count * width * tail_cache.shape[2]
    local_work = 4 * steps * count * width * prefix_cache.shape[1]
    keys, values, ancestors = call(
        prepare_kernel,
        [
            jax.ShapeDtypeStruct((count, tail_width, tail_cache.shape[2]), BF16),
            jax.ShapeDtypeStruct(tail_cache.shape[1:], BF16),
            jax.ShapeDtypeStruct(ancestors.shape, ancestors.dtype),
        ],
        [tail_cache, ancestors],
        0,
        spaces=[VMEM] * 2,
        scratch=(pltpu.SemaphoreType.DMA((2,)),),
    )
    answer = ancestors
    answers = []

    def reply_to(reach, parity, question, before):
        (answer,) = call(
            functools.partial(serve_kernel, length, reach, parity),
            [reply],
            [ancestors, question, keys, values, before],
            tail_work,
            spaces=[SMEM, VMEM, VMEM, VMEM, pl.ANY],
        )
        return answer

    for (reach, parity, pairs), question in zip(plans, asked):
        answer = reply_to(reach, parity, question, answer)
        answers.append(lax.ppermute(answer, both, pairs))
    answers.insert(0, reply_to(0, 0, queries, answer))
    local, logs = call(
        local_kernel,
        [jax.ShapeDtypeStruct(queries.shape, F32), jax.ShapeDtypeStruct((count, LANES), F32)],
        [queries, prefix_cache, fresh_kv],
        local_work,
        spaces=[VMEM] * 3,
    )
    repeats = jnp.sum(
        (sampled_ids[:, :, None] == prompt_ids[None, None, :]).astype(jnp.int32), axis=-1
    )
    looked_up = twist_table.at[sampled_ids].get(
        mode="promise_in_bounds", wrap_negative_indices=False
    )
    base = (looked_up - 2.0 * repeats.astype(F32)) * (1.0 / cores)
    attended, partial_value = call(
        functools.partial(combine_kernel, [plan[:2] for plan in plans]),
        [jax.ShapeDtypeStruct(queries.shape, BF16), jax.ShapeDtypeStruct((steps, count), F32)],
        [ancestors, local, logs, readout.reshape(1, width), base] + answers,
        16 * steps * count * width,
    )
    if cores == 2:
        twists = partial_value + lax.ppermute(partial_value, "tensor", [(0, 1), (1, 0)])
    else:
        twists = lax.psum(partial_value, "tensor")
    return (attended, twists)


def layer(length, *arguments):
    return on_device(length, *arguments)


def solution(mesh):
    return jax.shard_map(
        functools.partial(layer, mesh.shape["particle"]),
        mesh=mesh,
        in_specs=(
            P(None, "groups", "tensor"),
            P(None, ("groups", "particle"), None, "tensor"),
            P("groups"),
            P(None, ("groups", "particle"), "tensor"),
            P(None, None, ("groups", "particle"), "tensor"),
            P("groups"),
            P(None, ("groups", "particle")),
            P(),
            P("tensor"),
        ),
        out_specs=(P(None, ("groups", "particle"), "tensor"), P(None, ("groups", "particle"))),
        check_vma=False,
    )
```

```python
import functools
import math

import jax
import jax.numpy as jnp
from jax import lax
from jax.experimental import pallas as pl
from jax.experimental.pallas import tpu as pltpu
from jax.sharding import PartitionSpec as P


HEADS = 64
KV_HEADS = 8
HEAD = 128
EXCHANGES = ((1, 0), (2, 1), (2, 0), (1, 1))
SERVED = (0, 2, 1, 3)
GROUP = HEADS // KV_HEADS
EXPONENT_SCALE = math.log2(math.e) / math.sqrt(HEAD)

NEG_FILL = -1e30
LOG_STEPS = 32.0
LOG_FRACTION = 65534.0
TOP_CODE = 32000.0
TINY = 1e-30
LANES = 128

F32 = jnp.float32
BF16 = jnp.bfloat16
VMEM = pltpu.MemorySpace.VMEM
SMEM = pltpu.MemorySpace.SMEM


def exchanges(length, cores):
    found = []
    for reach, parity in EXCHANGES:
        partner = list(range(length))
        for i in range(length - reach):
            if (i // reach) % 2 == parity:
                partner[i], partner[i + reach] = i + reach, i
        pairs = []
        for i, other in enumerate(partner):
            turn = 1 if other == i else 0
            pairs += [(i * cores + c, other * cores + (c + turn) % cores) for c in range(cores)]
        found.append((reach, parity, pairs))
    return found


def partner_of(index, reach, parity):
    return jnp.where((index // reach) % 2 == parity, index + reach, index - reach)


def held_by(ancestors_ref, owner, holder, length, count):
    safe = jnp.clip(owner, 0, length - 1)
    exists = safe == owner
    found = []
    for p in range(count):
        slot = ancestors_ref[safe * count + p] - holder * count
        found.append((exists & (slot >= 0) & (slot < count), jnp.clip(slot, 0, count - 1)))
    return found


def head_tiles(query_ref, base):
    return [
        query_ref[t, :, base + g * HEAD : base + (g + 1) * HEAD].astype(F32)
        for t in range(query_ref.shape[0])
        for g in range(GROUP)
    ]


def scores_of(rows, keys):
    return lax.dot_general(rows, keys, (((1,), (1,)), ((), ())), preferred_element_type=F32)


def softmax_terms(scores):
    top = jnp.max(scores, axis=-1, keepdims=True)
    expo = jnp.exp2((scores - top) * EXPONENT_SCALE)
    return top, expo, jnp.sum(expo, axis=-1, keepdims=True)


def two_codes(value):
    value = value * LOG_STEPS
    whole = jnp.round(value)
    return whole, jnp.round((value - whole) * LOG_FRACTION)


def from_codes(whole, part):
    return (whole + part * (1.0 / LOG_FRACTION)) * (1.0 / LOG_STEPS)


def serve(slots, query_ref, key_ref, value_ref, out_ref):
    steps, count = query_ref.shape[0], query_ref.shape[1]
    heads = value_ref.shape[2] // HEAD
    many = steps * GROUP
    each = heads * many
    lane = lax.broadcasted_iota(jnp.int32, (GROUP, LANES), 1)
    row = lax.broadcasted_iota(jnp.int32, (GROUP, LANES), 0)
    notes = [[jnp.zeros((GROUP, LANES), F32) for _ in range(count)] for _ in range(3)]
    scores = []
    for k in range(heads):
        tiles = jnp.stack(head_tiles(query_ref, k * GROUP * HEAD), axis=0)
        rows = jnp.swapaxes(tiles, 0, 1).astype(BF16)
        cols = slice(k * HEAD, (k + 1) * HEAD)
        scores += [
            jnp.dot(rows[p], key_ref[slots[p], cols, :], preferred_element_type=F32)
            for p in range(count)
        ]
    terms = [softmax_terms(score) for score in scores]

    def note(which, p, k, column):
        for t in range(steps):
            here = lane == row + (k * many + t * GROUP)
            part = column[t * GROUP : (t + 1) * GROUP]
            notes[which][p] = jnp.where(here, part, notes[which][p])

    def gather_notes(which):
        return jnp.concatenate([jnp.sum(n, axis=0, keepdims=True) for n in notes[which]], axis=0)

    for k in range(heads):
        for p in range(count):
            top, _, total = terms[k * count + p]
            note(0, p, k, top)
            note(1, p, k, total)
    top, total = gather_notes(0), gather_notes(1)
    if each < LANES:
        total = jnp.maximum(total, TINY)
    spread = jnp.log2(total)
    level = two_codes(top * EXPONENT_SCALE + spread)
    outs = [
        jnp.dot(
            terms[k * count + p][1].astype(BF16),
            value_ref[slots[p], :, k * HEAD : (k + 1) * HEAD],
            preferred_element_type=F32,
        )
        for k in range(heads)
        for p in range(count)
    ]
    for k in range(heads):
        for p in range(count):
            out = outs[k * count + p]
            largest = jnp.maximum(jnp.max(jnp.abs(out), axis=-1, keepdims=True), TINY)
            code = jnp.round(out * (TOP_CODE / largest)).astype(jnp.int32)
            at = p * each + k * many
            out_ref[at : at + many, :] = code.astype(jnp.int16)
            note(2, p, k, largest)
    largest = gather_notes(2)
    if each < LANES:
        largest = jnp.maximum(largest, TINY)
    scale = two_codes(jnp.log2(largest) - spread - math.log2(TOP_CODE))
    coded = jnp.concatenate(level + scale, axis=0).astype(jnp.int32)
    out_ref[count * each :, :] = coded.astype(jnp.int16)


def serve_kernel(length, reach, parity, ancestors_ref, query_ref, key_ref, value_ref, _, out_ref):
    count = query_ref.shape[1]
    me = lax.axis_index("particle")
    asker = partner_of(me, reach, parity) if reach else me
    found = held_by(ancestors_ref, asker, me, length, count)
    serve([slot for _, slot in found], query_ref, key_ref, value_ref, out_ref)


def prepare_kernel(tail_ref, list_ref, key_ref, value_ref, list_out, sems):
    copies = [
        pltpu.make_async_copy(tail_ref.at[1], value_ref, sems.at[0]),
        pltpu.make_async_copy(list_ref, list_out, sems.at[1]),
    ]
    for copy in copies:
        copy.start()
    for j in range(tail_ref.shape[1]):
        for at in range(0, tail_ref.shape[3], HEAD):
            key_ref[j, at : at + HEAD, :] = tail_ref[0, j, :, at : at + HEAD].T
    for copy in copies:
        copy.wait()


def local_kernel(query_ref, prefix_ref, fresh_ref, out_ref, log_ref):
    steps, count = query_ref.shape[0], query_ref.shape[1]
    heads = prefix_ref.shape[2] // HEAD
    many = steps * GROUP
    lane = lax.broadcasted_iota(jnp.int32, (count, LANES), 1)
    logs = []
    for k in range(heads):
        cols = slice(k * HEAD, (k + 1) * HEAD)
        rows = jnp.concatenate(head_tiles(query_ref, k * GROUP * HEAD), axis=0).astype(BF16)
        top1, expo1, total1 = softmax_terms(scores_of(rows, prefix_ref[0, :, cols]))
        out1 = jnp.dot(expo1.astype(BF16), prefix_ref[1, :, cols], preferred_element_type=F32)
        fresh_keys = jnp.concatenate([fresh_ref[0, s, :, cols].astype(F32) for s in range(steps)], axis=0)
        fresh_values = jnp.concatenate([fresh_ref[1, s, :, cols].astype(F32) for s in range(steps)], axis=0)
        scores2 = scores_of(rows, fresh_keys.astype(BF16))
        row = lax.broadcasted_iota(jnp.int32, scores2.shape, 0)
        col = lax.broadcasted_iota(jnp.int32, scores2.shape, 1)
        seen = (row % count == col % count) & (col // count <= row // (GROUP * count))
        top2, expo2, total2 = softmax_terms(jnp.where(seen, scores2, NEG_FILL))
        out2 = jnp.dot(expo2.astype(BF16), fresh_values.astype(BF16), preferred_element_type=F32)
        top = jnp.maximum(top1, top2)
        share1 = jnp.exp2((top1 - top) * EXPONENT_SCALE)
        share2 = jnp.exp2((top2 - top) * EXPONENT_SCALE)
        total = share1 * total1 + share2 * total2
        context = (share1 * out1 + share2 * out2) / total
        context = context.reshape(many, count, HEAD)
        top, total = top.reshape(many, count, 1), total.reshape(many, count, 1)
        held = [jnp.zeros((count, LANES), F32) for _ in range(2)]
        for t in range(steps):
            for g in range(GROUP):
                at = (k * GROUP + g) * HEAD
                r = t * GROUP + g
                out_ref[t, :, at : at + HEAD] = context[r]
                held[0] = jnp.where(lane == k * many + r, top[r], held[0])
                held[1] = jnp.where(lane == k * many + r, total[r], held[1])
        inside = (lane >= k * many) & (lane < (k + 1) * many)
        level = held[0] * EXPONENT_SCALE + jnp.log2(jnp.where(inside, held[1], 1.0))
        logs.append(level)
    log_ref[...] = functools.reduce(jnp.add, logs)


def combine_kernel(plans, ancestors_ref, local_ref, log_ref, readout_ref, base_ref, *refs):
    sent_refs, (out_ref, twist_ref) = refs[: len(plans) + 1], refs[len(plans) + 1 :]
    steps, count = local_ref.shape[0], local_ref.shape[1]
    heads = local_ref.shape[2] // (HEAD * GROUP)
    many = steps * GROUP
    each = heads * many
    me = lax.axis_index("particle")
    source = []
    for p in range(count):
        parent = lax.div(ancestors_ref[me * count + p], count)
        found = jnp.int32(0)
        for m, (reach, parity) in enumerate(plans):
            found = jnp.where(parent == partner_of(me, reach, parity), m + 1, found)
        source.append(found)
    row = lax.broadcasted_iota(jnp.int32, (count, LANES), 0)
    lane = lax.broadcasted_iota(jnp.int32, (count, LANES), 1)

    def notes_of(ref):
        notes = ref[count * each :, :].astype(jnp.int32).astype(F32)
        return [notes[i * count : (i + 1) * count] for i in range(4)]

    sources = jnp.zeros((count, LANES), jnp.int32)
    for p in range(count):
        sources = jnp.where(row == p, source[p], sources)
    notes = notes_of(sent_refs[0])
    for m, ref in enumerate(sent_refs[1:], 1):
        notes = [jnp.where(sources == m, new, old) for new, old in zip(notes_of(ref), notes)]
    remote_level, scale = from_codes(*notes[:2]), from_codes(*notes[2:])
    local_level = log_ref[...]
    level = jnp.maximum(local_level, remote_level)
    local_share = jnp.exp2(local_level - level)
    remote_share = jnp.exp2(remote_level - level)
    total = local_share + remote_share
    local_share = local_share / total
    remote_share = remote_share / total * jnp.exp2(scale)
    gathered = [jnp.zeros((count, HEAD), F32) for _ in range(steps)]
    for k in range(heads):
        for pair in range(steps // 2):
            at = k * many + pair * 2 * GROUP
            picked = []
            for p in range(count):
                here = slice(p * each + at, p * each + at + 2 * GROUP)
                code = sent_refs[0][here, :]
                for m, ref in enumerate(sent_refs[1:], 1):
                    code = jnp.where(source[p] == m, ref[here, :], code)
                picked.append(code.astype(jnp.int32).astype(F32))
            tiles = jnp.swapaxes(jnp.stack(picked, axis=0), 0, 1)
            for r in range(2 * GROUP):
                t, h = pair * 2 + r // GROUP, k * GROUP + r % GROUP
                cols = slice(h * HEAD, (h + 1) * HEAD)
                context = local_share[:, at + r : at + r + 1] * local_ref[t, :, cols]
                context = context + remote_share[:, at + r : at + r + 1] * tiles[r]
                out_ref[t, :, cols] = context.astype(BF16)
                gathered[t] = gathered[t] + context * readout_ref[:, cols]
    for t in range(steps):
        column = jnp.sum(gathered[t], axis=-1, keepdims=True)
        line = jnp.sum(jnp.where(row == lane, column, 0.0), axis=0, keepdims=True)
        twist_ref[t : t + 1, :] = line[:, :count] + base_ref[t : t + 1, :]


def call(kernel, outs, operands, flops, spaces=None, scratch=(), limit=24 << 20):
    moved = sum(math.prod(o.shape) * o.dtype.itemsize for o in operands)
    moved += sum(math.prod(o.shape) * o.dtype.itemsize for o in outs)
    spaces = spaces or [SMEM] + [VMEM] * (len(operands) - 1)
    return pl.pallas_call(
        kernel,
        out_shape=tuple(outs),
        in_specs=[pl.BlockSpec(memory_space=space) for space in spaces],
        out_specs=tuple(pl.BlockSpec(memory_space=VMEM) for _ in outs),
        scratch_shapes=scratch,
        compiler_params=pltpu.CompilerParams(vmem_limit_bytes=limit),
        cost_estimate=pl.CostEstimate(flops=flops, bytes_accessed=moved, transcendentals=0),
    )(*operands)


def on_device(
    length,
    prefix_cache,
    tail_cache,
    ancestors,
    queries,
    fresh_kv,
    prompt_ids,
    sampled_ids,
    twist_table,
    readout,
):
    steps, count, width = queries.shape
    rows = steps * width // HEAD
    tail_width = tail_cache.shape[3]
    assert rows <= LANES and steps % 2 == 0
    cores = lax.axis_size("tensor")
    both = ("particle", "tensor")
    plans = exchanges(length, cores)
    asked = []
    for _, _, pairs in plans:
        asked.append(lax.ppermute(queries, both, pairs))
    reply = jax.ShapeDtypeStruct((count * rows + 4 * count, HEAD), jnp.int16)
    tail_work = 4 * steps * count * width * tail_cache.shape[2]
    local_work = 4 * steps * count * width * prefix_cache.shape[1]
    keys, values, ancestors = call(
        prepare_kernel,
        [
            jax.ShapeDtypeStruct((count, tail_width, tail_cache.shape[2]), BF16),
            jax.ShapeDtypeStruct(tail_cache.shape[1:], BF16),
            jax.ShapeDtypeStruct(ancestors.shape, ancestors.dtype),
        ],
        [tail_cache, ancestors],
        0,
        spaces=[VMEM] * 2,
        scratch=(pltpu.SemaphoreType.DMA((2,)),),
    )
    answer = ancestors
    answers = []

    def reply_to(reach, parity, question, before):
        (answer,) = call(
            functools.partial(serve_kernel, length, reach, parity),
            [reply],
            [ancestors, question, keys, values, before],
            tail_work,
            spaces=[SMEM, VMEM, VMEM, VMEM, pl.ANY],
        )
        return answer

    answers = [None] * (len(plans) + 1)
    for i in SERVED:
        reach, parity, pairs = plans[i]
        answer = reply_to(reach, parity, asked[i], answer)
        answers[i + 1] = lax.ppermute(answer, both, pairs)
    answers[0] = reply_to(0, 0, queries, answer)
    local, logs = call(
        local_kernel,
        [jax.ShapeDtypeStruct(queries.shape, F32), jax.ShapeDtypeStruct((count, LANES), F32)],
        [queries, prefix_cache, fresh_kv],
        local_work,
        spaces=[VMEM] * 3,
    )
    repeats = jnp.sum(
        (sampled_ids[:, :, None] == prompt_ids[None, None, :]).astype(jnp.int32), axis=-1
    )
    looked_up = twist_table.at[sampled_ids].get(
        mode="promise_in_bounds", wrap_negative_indices=False
    )
    base = (looked_up - 2.0 * repeats.astype(F32)) * (1.0 / cores)
    attended, partial_value = call(
        functools.partial(combine_kernel, [plan[:2] for plan in plans]),
        [jax.ShapeDtypeStruct(queries.shape, BF16), jax.ShapeDtypeStruct((steps, count), F32)],
        [ancestors, local, logs, readout.reshape(1, width), base] + answers,
        16 * steps * count * width,
    )
    if cores == 2:
        twists = partial_value + lax.ppermute(partial_value, "tensor", [(0, 1), (1, 0)])
    else:
        twists = lax.psum(partial_value, "tensor")
    return (attended, twists)


def layer(length, *arguments):
    return on_device(length, *arguments)


def solution(mesh):
    return jax.shard_map(
        functools.partial(layer, mesh.shape["particle"]),
        mesh=mesh,
        in_specs=(
            P(None, "groups", "tensor"),
            P(None, ("groups", "particle"), None, "tensor"),
            P("groups"),
            P(None, ("groups", "particle"), "tensor"),
            P(None, None, ("groups", "particle"), "tensor"),
            P("groups"),
            P(None, ("groups", "particle")),
            P(),
            P("tensor"),
        ),
        out_specs=(P(None, ("groups", "particle"), "tensor"), P(None, ("groups", "particle"))),
        check_vma=False,
    )
```
